256 devices in a mesh: seq: 16 (over x_hi, y, core), head: 16 (over x_lo, z).
Axes of the slice: x: 4 (x_hi: 2, x_lo: 2; x = x_hi * 2 + x_lo), y: 4, z: 8, core: 2. Of those that a mesh axis runs over, the one named last changes fastest.
Arguments:
- grad_out: bfloat16 [4096, 8192], P('seq', 'head'), may hold values from -6 to 6
- out_weight: bfloat16 [16384, 8192], P('head', 'seq'), may hold values from -0.046875 to 0.046875
- ssm_input: bfloat16 [4096, 16384], P('seq', 'head'), may hold values from -6 to 6
- step_size: float32 [4096, 128], P('seq', 'head'), may hold values from 0.02 to 0.2
- log_decay: float32 [4096, 128], P('seq', 'head'), may hold values from -1 to 0, as said below
- b_in: bfloat16 [4096, 256], P('seq'), may hold values from -1.5 to 1.5
- c_in: bfloat16 [4096, 256], P('seq'), may hold values from -1.5 to 1.5
- skip: float32 [128], P('head'), may hold values from 0.5 to 1.5
Outputs:
- grad_input: bfloat16 [4096, 16384], P('seq', 'head')
- grad_step: float32 [4096, 128], P('seq', 'head')
- grad_decay: float32 [4096, 128], P('seq', 'head')
- grad_b: float32 [4096, 256], P('seq')
- grad_c: float32 [4096, 256], P('seq')
The draws below stay inside these ranges and needn't reach their ends.
Inputs may be any that keep to these rules, and one draw needn't show every extreme that they name: `log_decay`: every entry is negative.
All inputs are finite; a program needn't handle non-finite values.
Results may differ from the reference program's by a relative error of at most 0.0049.
Values may be sent and summed in bfloat16 or wider, within the bound.
A program may use at most 64 MiB of HBM per device.

```python
import math
import jax
import jax.numpy as jnp
from jax import lax

D = 8192
SPACE_HEADS = 128
HEAD_DIM = 128
STATE = 256
TOK_DEV = 256
SEQUENCE_TOKENS = 4096
INNER = 16384


def draw_log_decay(key, part):
    random_subkeys = [jax.random.fold_in(key, 11 + draw_index) for draw_index in range(6)]
    slow_share = 0.5
    is_slow = jax.random.uniform(random_subkeys[0], (SPACE_HEADS,)) < slow_share
    fast_rate = jax.random.uniform(random_subkeys[1], (SPACE_HEADS,), minval=1.0 / 50.0, maxval=1.0 / 30.0)
    baseline_rate = jnp.where(is_slow, 0.35 / SEQUENCE_TOKENS, fast_rate)
    block_count = SEQUENCE_TOKENS // TOK_DEV
    block_multiplier = jnp.exp(jax.random.uniform(random_subkeys[2], (block_count, SPACE_HEADS), minval=math.log(0.6), maxval=math.log(1.6)))
    block_multiplier = jnp.repeat(block_multiplier, TOK_DEV, axis=0)
    jaggedness_level = jax.random.uniform(random_subkeys[3], (SEQUENCE_TOKENS, SPACE_HEADS), minval=0.5, maxval=1.5)
    token_positions = jax.random.randint(random_subkeys[4], (3, SPACE_HEADS), 0, SEQUENCE_TOKENS)
    row_indices = lax.broadcasted_iota(jnp.int32, (SEQUENCE_TOKENS, 3, SPACE_HEADS), 0)
    surge_events = jnp.any(row_indices == token_positions[None], axis=1).astype(jnp.float32)
    surge_length = jax.random.uniform(random_subkeys[5], (SEQUENCE_TOKENS, SPACE_HEADS), minval=0.22, maxval=0.69)
    return -(baseline_rate[None, :] * block_multiplier * jaggedness_level + surge_events * surge_length)


def block_scale(own_key, extent, pieces, least, high):
    level, own = 1.0, jax.random.fold_in(own_key, 6)
    for axis_at, shards_of in pieces:
        steps = jnp.exp(jax.random.uniform(jax.random.fold_in(own, axis_at), (shards_of,), jnp.float32, least / len(pieces), high / len(pieces)))
        level = level * jnp.repeat(steps, extent[axis_at] // shards_of).reshape([-1 if axis == axis_at else 1 for axis in range(len(extent))])
    return level


def bell_draw(own_key, shape, spread, most, split=(), dtype=jnp.bfloat16):
    array = jax.random.normal(own_key, shape, jnp.float32) * spread
    if len(split) > 0:
        array = block_scale(own_key, shape, split, -0.22, 0.18) * array
    return jnp.clip(array, min=-most, max=most).astype(dtype)


def setup_inputs(seed: int = 0) -> dict:
    key_of = jax.random.split(jax.random.key(seed), 9)
    return {
        "grad_out": bell_draw(key_of[0], (SEQUENCE_TOKENS, D), 1.0, 6.0, ((0, 16), (1, 16))),
        "out_weight": bell_draw(key_of[1], (INNER, D), INNER ** -0.5, 0.046875, ((0, 16), (1, 16))),
        "ssm_input": bell_draw(key_of[2], (SEQUENCE_TOKENS, INNER), 1.0, 6.0, ((0, 16), (1, 16))),
        "step_size": jnp.clip(jnp.exp(math.log(0.2) - 2.3025851 * jax.random.uniform(key_of[3], (SEQUENCE_TOKENS, SPACE_HEADS), jnp.float32) ** block_scale(key_of[3], (SEQUENCE_TOKENS, SPACE_HEADS), ((0, 16), (1, 16)), -0.2, 0.2)), 0.02, 0.2),
        "log_decay": draw_log_decay(jax.random.fold_in(key_of[8], 71), 0),
        "b_in": bell_draw(key_of[5], (SEQUENCE_TOKENS, STATE), 0.25, 1.5, ((0, 16),)),
        "c_in": bell_draw(key_of[6], (SEQUENCE_TOKENS, STATE), 0.25, 1.5, ((0, 16),)),
        "skip": jnp.clip(0.5 + 1.0 * jax.random.uniform(key_of[7], (SPACE_HEADS,), jnp.float32) ** block_scale(key_of[7], (SPACE_HEADS,), ((0, 16),), -0.2, 0.2), 0.5, 1.5),
    }


HIGH = lax.Precision.HIGHEST

def inner_terms(inputs, strides, running, b_rows, c_rows, skips):
    span = inputs.shape[0]
    row_pos = lax.broadcasted_iota(jnp.int32, (span, span), 0)
    col_pos = lax.broadcasted_iota(jnp.int32, (span, span), 1)
    causal = row_pos >= col_pos
    running_t = running.T
    gaps = running_t[:, :, None] - running_t[:, None, :]
    weights = jnp.exp(jnp.where(causal[None], gaps, -jnp.inf)) * strides.T[:, None, :]
    intersection = jnp.dot(c_rows, b_rows.T, precision=HIGH)
    mixed_sum = jnp.einsum('hts,shp->thp', weights * intersection[None], inputs, precision=HIGH)
    return mixed_sum + skips[None, :, None] * inputs

def carried(c_rows, running, carried_state):
    readout = jnp.einsum('tn,hpn->thp', c_rows, carried_state, precision=HIGH)
    return readout * jnp.exp(running)[:, :, None]

def closing(inputs, strides, b_rows, running, carried_state):
    block_end = running[-1]
    input_scale = strides * jnp.exp(block_end[None, :] - running)
    fresh = jnp.einsum('thp,tn->hpn', inputs * input_scale[:, :, None], b_rows, precision=HIGH)
    return jnp.exp(block_end)[:, None, None] * carried_state + fresh

def block_forward(inputs, strides, decays, b_rows, c_rows, skips, carried_state):
    running = jnp.cumsum(decays, axis=0)
    outputs = inner_terms(inputs, strides, running, b_rows, c_rows, skips) + carried(c_rows, running, carried_state)
    return (outputs, closing(inputs, strides, b_rows, running, carried_state))

def reference(grad_out, out_weight, ssm_input, step_size, log_decay, b_in, c_in, skip):
    summed = lax.dot_general(grad_out, out_weight, (((1,), (1,)), ((), ())), preferred_element_type=jnp.float32)
    grad_y = summed.astype(jnp.bfloat16)
    block_count = SEQUENCE_TOKENS // TOK_DEV

    def by_blocks(values):
        return values.reshape((block_count, TOK_DEV) + values.shape[1:])

    def forward(inputs, strides, decays, b_rows, c_rows):

        def advance(carried_state, block_inputs):
            outputs, ending = block_forward(block_inputs[0], block_inputs[1], block_inputs[2], block_inputs[3], block_inputs[4], skip, carried_state)
            return (ending, outputs)
        initial = jnp.zeros((SPACE_HEADS, HEAD_DIM, STATE), jnp.float32)
        _, outputs = lax.scan(jax.checkpoint(advance), initial, (by_blocks(inputs), by_blocks(strides), by_blocks(decays), by_blocks(b_rows), by_blocks(c_rows)))
        return outputs.reshape(SEQUENCE_TOKENS, SPACE_HEADS, HEAD_DIM)
    inputs = ssm_input.astype(jnp.float32).reshape(SEQUENCE_TOKENS, SPACE_HEADS, HEAD_DIM)
    _, pull_back = jax.vjp(forward, inputs, step_size, log_decay, b_in.astype(jnp.float32), c_in.astype(jnp.float32))
    gradients = pull_back(grad_y.astype(jnp.float32).reshape(SEQUENCE_TOKENS, SPACE_HEADS, HEAD_DIM))
    grad_input = gradients[0].reshape(SEQUENCE_TOKENS, INNER).astype(jnp.bfloat16)
    return (grad_input, gradients[1], gradients[2], gradients[3], gradients[4])
```

```python
import jax
import jax.numpy as jnp
from jax import lax
from jax.experimental import pallas as pl
from jax.experimental.pallas import tpu as pltpu
from jax.sharding import PartitionSpec as P

F32, BF16 = jnp.float32, jnp.bfloat16
HIGH = lax.Precision.HIGHEST
NN = (((1,), (0,)), ((), ()))
NT = (((1,), (1,)), ((), ()))
TN = (((0,), (0,)), ((), ()))

TOK = 256
HEADS = 8
WIDTH = 128
STATE = 256
ROWS = HEADS * WIDTH
COLS = 512
GROUP = 16
SLICE = ROWS // GROUP
PART = TOK // GROUP
CUT = 608


def mm(a, b, dims):
    return lax.dot_general(a, b, dims, preferred_element_type=F32)


def exact(a, b, dims):
    return lax.dot_general(a, b, dims, precision=HIGH, preferred_element_type=F32)


def split(a):
    high = a.astype(BF16)
    return high, (a - high.astype(F32)).astype(BF16)


def remote(src, dst, send_sem, recv_sem, seq, head):
    return pltpu.make_async_remote_copy(
        src_ref=src,
        dst_ref=dst,
        send_sem=send_sem,
        recv_sem=recv_sem,
        device_id={"seq": seq, "head": head},
        device_id_type=pl.DeviceIdType.MESH,
    )


LOW, TOP = (0, CUT), (CUT, ROWS)
LOW0, LOW1 = (0, CUT // 2), (CUT // 2, CUT)
TOP0, TOP1 = (CUT, (CUT + ROWS) // 2), ((CUT + ROWS) // 2, ROWS)
HOPS = {
    "b1": (0, 0, TOP, "up"),
    "b2": (0, 0, TOP, "down"),
    "b0": (0, 0, TOP, "x"),
    "a1": (0, 0, LOW, "up"),
    "a2": (0, 0, LOW, "down"),
    "a0": (0, 0, LOW, "x"),
    "b5": (0, -1, TOP0, "up"),
    "b7": (0, -1, TOP, "x"),
    "b6": (0, 1, TOP1, "down"),
    "b8": (0, 1, TOP, "x"),
    "b9": (0, 2, TOP0, "x"),
    "b10": (0, 2, TOP1, "x"),
    "a5": (0, -1, LOW0, "up"),
    "a6": (0, 1, LOW1, "down"),
    "a3": (1, 0, LOW, "up"),
    "a4": (1, 0, LOW, "down"),
    "a7": (1, -1, LOW0, "up"),
    "a8": (1, 1, LOW1, "down"),
}
HOP_AT = {name: at for at, name in enumerate(HOPS)}


def kernel(
    go_ref, w_ref, x_ref, dt_ref, ld_ref, b_ref, c_ref, skip_ref,
    gi_ref, gs_ref, gd_ref, gb_ref, gc_ref,
    wbuf, gbuf, acc, pbuf, gy, ge, xs, dxs, cb, vsum, urow, dcol, qcol, dtile, decs,
    sfw, rfw, ofw, hbuf, sbw, rbw, obw, qbuf, dcp, dbp, prc, prb, gcs, gbs,
    w_s, w_r, g_s, g_r, z_s, z_r, p_s, p_r, e_s, e_r, f_s, f_r, h_s, h_r, l_s, l_r, q_s, q_r,
    rc_s, rc_r, ac_s, ac_r, rb_s, rb_r, ab_s, ab_r,
):
    seq = lax.axis_index("seq")
    head = lax.axis_index("head")
    xh = lax.div(seq, 8)
    yy = lax.rem(lax.div(seq, 2), 4)
    core = lax.rem(seq, 2)
    xl = lax.div(head, 8)
    zz = lax.rem(head, 8)
    other = seq + 1 - 2 * core
    beside = (1 - xl) * 8 + zz
    home = lax.rem(zz, 2)
    odd = lax.rem(zz + core, 2)

    barrier = pltpu.get_barrier_semaphore()

    def greet(s, h):
        pl.semaphore_signal(
            barrier, inc=1, device_id={"seq": s, "head": h}, device_id_type=pl.DeviceIdType.MESH
        )

    for d in range(1, GROUP):
        greet(lax.rem(seq + d, GROUP), head)
        greet(seq, lax.rem(head + d, GROUP))
    greet(other, beside)
    pl.semaphore_wait(barrier, 2 * (GROUP - 1) + 1)

    sent = []

    def start(copy):
        copy.start()
        sent.append(copy)

    def shard(dx, dy):
        x_at = xh if dx == 0 else 1 - xh
        return x_at * 4 + lax.rem(yy + dy + 4, 4)

    def hop(name):
        dx, dy, (lo, hi), way = HOPS[name]
        at = HOP_AT[name]
        where = pl.ds(lo, hi - lo)
        slot = wbuf.at[shard(dx, dy), where]
        src = w_ref.at[where] if (dx, dy) == (0, 0) else slot
        if way == "x":
            to = (1 - xh) * 8 + yy * 2 + core
        else:
            to = xh * 8 + lax.rem(yy + (1 if way == "up" else 3), 4) * 2 + core
        return remote(src, slot, w_s.at[at], w_r.at[at], to, head)

    def go(*names):
        for name in names:
            start(hop(name))

    def got(*names):
        for name in names:
            dx, dy, (lo, hi), way = HOPS[name]
            at = HOP_AT[name]
            if way == "x":
                dx = 1 - dx
            else:
                dy = dy - 1 if way == "up" else dy + 1
            slot = wbuf.at[shard(dx, dy), pl.ds(lo, hi - lo)]
            remote(slot, slot, w_s.at[at], w_r.at[at], seq, head).wait_recv()

    home_seq = seq - core + home
    own_at = xl * 4 + lax.div(zz, 2)
    beside_at = (1 - xl) * 4 + lax.div(zz, 2)
    across = remote(go_ref, gbuf.at[own_at, core], g_s.at[0], g_r.at[core], home_seq, beside)
    start(across)
    to_other = remote(go_ref, gbuf.at[own_at, core], g_s.at[1], g_r.at[2], other, head)

    @pl.when(odd == 1)
    def _():
        to_other.start()

    go("b1", "b2", "b0", "a1", "a2", "a0")

    @pl.when(odd == 0)
    def _():
        gbuf[own_at, core] = go_ref[...]

    def unit(x_at, way, d, half):
        z_from = lax.rem(zz + (8 - d if way == 0 else d), 8)
        k = x_at * 4 + lax.div(z_from, 2)
        return gbuf.at[k, way] if half else gbuf.at[k]

    def z_hop(way, stage, x_at, is_odd):
        part = unit(x_at, way, 2 * stage + is_odd, is_odd and stage == 1)
        z_to = lax.rem(zz + (1 if way == 0 else 7), 8)
        return remote(
            part, part, z_s.at[way, stage, x_at], z_r.at[way, stage, x_at], seq, xl * 8 + z_to
        )

    def z_got(way, stage, x_at, is_odd):
        part = unit(x_at, way, 2 * stage + (1 if is_odd else 2), (not is_odd) and stage == 1)
        remote(
            part, part, z_s.at[way, stage, x_at], z_r.at[way, stage, x_at], seq, head
        ).wait_recv()

    pairs = [(way, x_at) for x_at in range(2) for way in range(2)]

    def z_start(stage, is_odd):
        for way, x_at in pairs:
            z_hop(way, stage, x_at, is_odd).start()

    def z_pass(stage_in, stage_out, is_odd):
        for way, x_at in pairs:
            z_got(way, stage_in, x_at, is_odd)
            if stage_out is not None:
                z_hop(way, stage_out, x_at, is_odd).start()

    rows_i = lax.broadcasted_iota(jnp.int32, (TOK, TOK), 0)
    cols_i = lax.broadcasted_iota(jnp.int32, (TOK, TOK), 1)
    causal = rows_i >= cols_i
    lower = jnp.where(causal, 1.0, 0.0).astype(F32)
    upper = jnp.where(rows_i <= cols_i, 1.0, 0.0).astype(F32)
    eye = jnp.where(rows_i == cols_i, 1.0, 0.0).astype(F32)
    lane = lax.broadcasted_iota(jnp.int32, (TOK, HEADS), 1)
    lane1 = lax.broadcasted_iota(jnp.int32, (1, HEADS), 1)
    dt = dt_ref[...]
    ld = ld_ref[...]
    run = exact(lower, ld, NN)
    run_row = exact(ld, upper, TN)
    dt_row = exact(dt, eye, TN)
    end = run[TOK - 1 : TOK, :]
    fade = jnp.exp(end - run)
    scale = dt * fade
    rise = jnp.exp(run)
    exp_end = jnp.exp(end)

    b_all = b_ref[...]
    c_all = c_ref[...]
    for h in range(HEADS):
        ch = slice(h * WIDTH, (h + 1) * WIDTH)
        scaled = x_ref[:, ch].astype(F32) * scale[:, h : h + 1]
        part, rest = split(scaled)
        xs[:, ch] = part
        made = mm(part, b_all, TN) + mm(rest, b_all, TN)
        sfw[2 * h : 2 * h + 2] = made.reshape(2, SLICE, STATE)
        dtile[h] = jnp.broadcast_to(exp_end[:, h : h + 1], (8, 128))

    def to_seq(src, dst, ss, rs):
        for d in range(1, GROUP):
            peer = lax.rem(seq + d, GROUP)
            start(remote(src.at[peer], dst.at[seq], ss.at[d], rs.at[d], peer, head))
        dst[seq] = src[seq]

    def from_seq(dst, ss, rs):
        for d in range(1, GROUP):
            peer = lax.rem(seq + GROUP - d, GROUP)
            remote(dst.at[peer], dst.at[peer], ss.at[d], rs.at[d], seq, head).wait_recv()

    for d in range(1, GROUP):
        peer = lax.rem(seq + d, GROUP)
        start(remote(dtile.at[lax.div(peer, 2)], decs.at[seq], e_s.at[d], e_r.at[d], peer, head))
    decs[seq] = dtile[lax.div(seq, 2)]
    to_seq(sfw, rfw, f_s, f_r)

    @pl.when(odd == 0)
    def _():
        for i, at in enumerate((beside_at, beside_at, own_at)):
            tok = i if i < 2 else 1 - core
            slot = gbuf.at[at, tok]
            remote(slot, slot, g_s.at[0], g_r.at[i], seq, head).wait_recv()
        z_start(0, 0)

    cb[...] = mm(c_all, b_all, NT)

    got("b1")
    go("b7", "b5")
    got("b2")
    go("b8", "b6")

    @pl.when(odd == 1)
    def _():
        z_pass(0, 0, 1)

    got("b5")
    go("b9")
    got("b6")
    go("b10")
    got("a1")
    go("a5")
    got("a2")
    go("a6")
    got("a0")
    go("a3", "a4")

    def scan(order, inbox, outbox):
        state = jnp.zeros((SLICE, STATE), F32)
        for s in order:
            outbox[s] = state
            state = state * decs[s, 0:1, 0:1] + inbox[s]

    from_seq(decs, e_s, e_r)
    from_seq(rfw, f_s, f_r)
    scan(range(GROUP), rfw, ofw)
    to_seq(ofw, hbuf, h_s, h_r)

    @pl.when(odd == 0)
    def _():
        z_pass(0, 1, 0)

    got("a3")
    go("a7")
    got("a4")
    go("a8")

    @pl.when(odd == 1)
    def _():
        z_pass(1, 1, 1)

    @pl.when(odd == 0)
    def _():
        z_pass(1, None, 0)

    def block(at, weights, first):
        left = gbuf[at].reshape(2 * TOK, COLS)
        for n in range(4):
            col = slice(n * 256, (n + 1) * 256)
            new = mm(left, weights(n), NT)
            acc[:, col] = new if first else acc[:, col] + new

    def held(dx, dy):
        at = shard(dx, dy)
        return at, lambda n: wbuf[at, n * 256 : (n + 1) * 256, :]

    block(shard(0, 0), lambda n: w_ref[n * 256 : (n + 1) * 256, :], True)
    got("b0")
    block(*held(1, 0), False)
    block(*held(0, -1), False)
    block(*held(0, 1), False)
    got("a5", "a6")
    block(*held(0, 2), False)
    from_seq(hbuf, h_s, h_r)
    got("b7")
    block(*held(1, -1), False)
    got("b8")
    block(*held(1, 1), False)
    got("b9", "b10", "a7", "a8")
    block(*held(1, 2), False)

    mine = pl.ds(pl.multiple_of(core * TOK, TOK), TOK)
    theirs = pl.ds(pl.multiple_of((1 - core) * TOK, TOK), TOK)
    swap = remote(acc.at[theirs], pbuf, p_s.at[0], p_r.at[0], other, head)
    start(swap)
    swap.wait_recv()
    for h in range(HEADS):
        ch = slice(h * WIDTH, (h + 1) * WIDTH)
        up = (acc[mine, ch] + pbuf[:, ch]).astype(BF16)
        gy[:, ch] = up
        part, rest = split(up.astype(F32) * rise[:, h : h + 1])
        ge[:, ch] = part
        made = mm(part, c_all, TN) + mm(rest, c_all, TN)
        sbw[2 * h : 2 * h + 2] = made.reshape(2, SLICE, STATE)
    to_seq(sbw, rbw, l_s, l_r)

    vsum[...] = jnp.zeros((TOK, TOK), F32)
    dcol[...] = jnp.zeros((TOK, HEADS), F32)

    def inner(h):
        ch = slice(h * WIDTH, (h + 1) * WIDTH)
        up = gy[:, ch]
        gx = mm(up, x_ref[:, ch], NT)
        gaps = run[:, h : h + 1] - run_row[h : h + 1, :]
        decay = jnp.exp(jnp.where(causal, gaps, -1e30))
        steps = dt_row[h : h + 1, :]
        mixed = decay * cb[...]
        both = mixed * gx
        vsum[...] += decay * gx * steps
        urow[h : h + 1, :] = jnp.sum(both, axis=0, keepdims=True)
        along = jnp.sum(both * steps, axis=1, keepdims=True)
        dxs[:, ch] = mm((mixed * steps).astype(BF16), up, TN)
        part, rest = split(hbuf[2 * h : 2 * h + 2].reshape(WIDTH, STATE))
        read = mm(c_all, part, NT) + mm(c_all, rest, NT)
        along += rise[:, h : h + 1] * jnp.sum(up.astype(F32) * read, axis=1, keepdims=True)
        dcol[...] += jnp.where(lane == h, along, 0.0)

    for h in range(HEADS // 2):
        inner(h)

    from_seq(rbw, l_s, l_r)
    scan(range(GROUP - 1, -1, -1), rbw, obw)
    to_seq(obw, qbuf, q_s, q_r)

    for h in range(HEADS // 2, HEADS):
        inner(h)

    v_hi = vsum[...].astype(BF16)
    v_lo = (vsum[...] - v_hi.astype(F32)).astype(BF16)

    def spread(src, dst, ss, rs):
        for d in range(1, GROUP):
            peer = lax.rem(head + d, GROUP)
            part = src.at[pl.ds(pl.multiple_of(peer * PART, PART), PART)]
            start(remote(part, dst.at[head], ss.at[d], rs.at[d], seq, peer))
        dst[head] = src[pl.ds(pl.multiple_of(head * PART, PART), PART)]

    def collect(inbox, whole, ss, rs, ss2, rs2):
        for d in range(1, GROUP):
            peer = lax.rem(head + GROUP - d, GROUP)
            remote(inbox.at[peer], inbox.at[peer], ss.at[d], rs.at[d], seq, head).wait_recv()
        total = inbox[0]
        for i in range(1, GROUP):
            total = total + inbox[i]
        own = pl.ds(pl.multiple_of(head * PART, PART), PART)
        whole[own] = total
        for d in range(1, GROUP):
            peer = lax.rem(head + d, GROUP)
            start(remote(whole.at[own], whole.at[own], ss2.at[d], rs2.at[d], seq, peer))

    def finish(whole, out, ss, rs):
        for d in range(1, GROUP):
            peer = lax.rem(head + GROUP - d, GROUP)
            part = whole.at[pl.ds(pl.multiple_of(peer * PART, PART), PART)]
            remote(part, part, ss.at[d], rs.at[d], seq, head).wait_recv()
        out[...] = whole[...]

    dcp[...] = (
        mm(v_hi, b_all, NN)
        + mm(v_lo, b_all, NN)
        + mm(ge[...], hbuf[...].reshape(ROWS, STATE).astype(BF16), NN)
    )
    spread(dcp, prc, rc_s, rc_r)
    dbp[...] = mm(v_hi, c_all, TN) + mm(v_lo, c_all, TN)
    u_col = exact(eye, urow[...], NT)

    from_seq(qbuf, q_s, q_r)
    dbp[...] += mm(xs[...], qbuf[...].reshape(ROWS, STATE).astype(BF16), NN)
    spread(dbp, prb, rb_s, rb_r)
    collect(prc, gcs, rc_s, rc_r, ac_s, ac_r)

    qcol[...] = jnp.zeros((TOK, HEADS), F32)
    inner_hq = jnp.zeros((1, HEADS), F32)
    for h in range(HEADS // 2):
        inner_hq = closing(h, lane, lane1, b_all, x_ref, gy, dxs, hbuf, qbuf, qcol, scale, skip_ref, gi_ref, inner_hq)
    collect(prb, gbs, rb_s, rb_r, ab_s, ab_r)
    for h in range(HEADS // 2, HEADS):
        inner_hq = closing(h, lane, lane1, b_all, x_ref, gy, dxs, hbuf, qbuf, qcol, scale, skip_ref, gi_ref, inner_hq)

    step_grad = u_col + fade * qcol[...]
    gs_ref[...] = step_grad
    at_end = jnp.sum(scale * qcol[...], axis=0, keepdims=True) + exp_end * inner_hq
    gd_ref[...] = exact(upper, dcol[...] - dt * step_grad, NN) + at_end

    finish(gcs, gc_ref, ac_s, ac_r)
    finish(gbs, gb_ref, ab_s, ab_r)

    for copy in sent:
        copy.wait_send()

    @pl.when(odd == 1)
    def _():
        to_other.wait_send()
        for stage in range(2):
            for way, x_at in pairs:
                z_hop(way, stage, x_at, 1).wait_send()

    @pl.when(odd == 0)
    def _():
        for stage in range(2):
            for way, x_at in pairs:
                z_hop(way, stage, x_at, 0).wait_send()


def closing(h, lane, lane1, b_all, x_ref, gy, dxs, hbuf, qbuf, qcol, scale, skip_ref, gi_ref, inner_hq):
    ch = slice(h * WIDTH, (h + 1) * WIDTH)
    grad = qbuf[2 * h : 2 * h + 2].reshape(WIDTH, STATE)
    part, rest = split(grad)
    fed = mm(b_all, part, NT) + mm(b_all, rest, NT)
    met = jnp.sum(x_ref[:, ch].astype(F32) * fed, axis=1, keepdims=True)
    qcol[...] += jnp.where(lane == h, met, 0.0)
    gi_ref[:, ch] = (
        dxs[:, ch]
        + skip_ref[:, h : h + 1] * gy[:, ch].astype(F32)
        + scale[:, h : h + 1] * fed
    ).astype(BF16)
    state = hbuf[2 * h : 2 * h + 2].reshape(WIDTH, STATE)
    prod = state * grad
    total = jnp.sum(jnp.sum(prod, axis=0, keepdims=True), axis=1, keepdims=True)
    return inner_hq + jnp.where(lane1 == h, total, 0.0)


def local(grad_out, out_weight, ssm_input, step_size, log_decay, b_in, c_in, skip):
    vmem = pl.BlockSpec(memory_space=pltpu.VMEM)
    dma = pltpu.SemaphoreType.DMA
    slices = pltpu.VMEM((GROUP, SLICE, STATE), F32)
    parts = pltpu.VMEM((GROUP, PART, STATE), F32)
    square = pltpu.VMEM((TOK, STATE), F32)
    by_head = pltpu.VMEM((TOK, HEADS), F32)
    wide = pltpu.VMEM((TOK, ROWS), BF16)
    peers = dma((GROUP,))
    return pl.pallas_call(
        kernel,
        out_shape=(
            jax.ShapeDtypeStruct((TOK, ROWS), BF16),
            jax.ShapeDtypeStruct((TOK, HEADS), F32),
            jax.ShapeDtypeStruct((TOK, HEADS), F32),
            jax.ShapeDtypeStruct((TOK, STATE), F32),
            jax.ShapeDtypeStruct((TOK, STATE), F32),
        ),
        in_specs=[vmem] * 8,
        out_specs=[vmem] * 5,
        scratch_shapes=[
            pltpu.VMEM((8, ROWS, COLS), BF16),
            pltpu.VMEM((8, 2, TOK, COLS), BF16),
            pltpu.VMEM((2 * TOK, ROWS), F32),
            pltpu.VMEM((TOK, ROWS), F32),
            wide,
            wide,
            wide,
            pltpu.VMEM((TOK, ROWS), F32),
            pltpu.VMEM((TOK, TOK), F32),
            pltpu.VMEM((TOK, TOK), F32),
            pltpu.VMEM((HEADS, TOK), F32),
            by_head,
            by_head,
            pltpu.VMEM((HEADS, 8, 128), F32),
            pltpu.VMEM((GROUP, 8, 128), F32),
            slices, slices, slices, slices,
            slices, slices, slices, slices,
            square, square,
            parts, parts,
            square, square,
            dma((len(HOPS),)), dma((len(HOPS),)),
            dma((2,)), dma((3,)),
            dma((2, 2, 2)), dma((2, 2, 2)),
            dma((1,)), dma((1,)),
        ] + [peers] * 18,
        compiler_params=pltpu.CompilerParams(
            collective_id=0, has_side_effects=True, vmem_limit_bytes=52 * 2**20
        ),
        name="layer_backward",
    )(grad_out, out_weight, ssm_input, step_size, log_decay, b_in, c_in, skip.reshape(1, HEADS))


def solution(mesh):
    in_specs = (
        P("seq", "head"),
        P("head", "seq"),
        P("seq", "head"),
        P("seq", "head"),
        P("seq", "head"),
        P("seq", None),
        P("seq", None),
        P("head"),
    )
    out_specs = (
        P("seq", "head"),
        P("seq", "head"),
        P("seq", "head"),
        P("seq", None),
        P("seq", None),
    )
    return jax.shard_map(local, mesh=mesh, in_specs=in_specs, out_specs=out_specs, check_vma=False)
```

```python
import jax
import jax.numpy as jnp
from jax import lax
from jax.experimental import pallas as pl
from jax.experimental.pallas import tpu as pltpu
from jax.sharding import PartitionSpec as P

F32, BF16 = jnp.float32, jnp.bfloat16
HIGH = lax.Precision.HIGHEST
NN = (((1,), (0,)), ((), ()))
NT = (((1,), (1,)), ((), ()))
TN = (((0,), (0,)), ((), ()))

TOK = 256
HEADS = 8
WIDTH = 128
STATE = 256
ROWS = HEADS * WIDTH
COLS = 512
GROUP = 16
CHIPS = 8
SLICE = ROWS // GROUP
PART = TOK // GROUP
HALF = ROWS // 2
CHUNKS = 4
WIDE = ROWS // CHUNKS


def mm(a, b, dims):
    return lax.dot_general(a, b, dims, preferred_element_type=F32)


def exact(a, b, dims):
    return lax.dot_general(a, b, dims, precision=HIGH, preferred_element_type=F32)


def split(a):
    high = a.astype(BF16)
    return high, (a - high.astype(F32)).astype(BF16)


def remote(src, dst, send_sem, recv_sem, seq, head):
    return pltpu.make_async_remote_copy(
        src_ref=src,
        dst_ref=dst,
        send_sem=send_sem,
        recv_sem=recv_sem,
        device_id={"seq": seq, "head": head},
        device_id_type=pl.DeviceIdType.MESH,
    )


HOPS = {
    "u0": (0, 0, "up"),
    "d1": (0, HALF, "down"),
    "u1": (0, HALF, "up"),
    "d0": (0, 0, "down"),
    "f0": (-1, 0, "up"),
    "f1": (1, HALF, "down"),
}
HOP_AT = {name: at for at, name in enumerate(HOPS)}


def kernel(
    go_hbm, w_hbm, x_hbm, dt_hbm, ld_hbm, b_hbm, c_hbm, skip_hbm,
    gi_ref, gs_ref, gd_ref, gb_ref, gc_ref,
    x_ref, dt_ref, ld_ref, b_ref, c_ref, skip_ref, in_s,
    wbuf, gbuf, accp, acco, pbufp, pbufo, xout, xin, gy, ge, xs, xs_low, wts, dxs, cb, vsum, urow, dcol, qcol, dtile, dother,
    sfw, hin, hpair, rfw, ofw, hback, hsend, hbuf,
    sbw, qin, qpair, rbw, obw, qback, qsend, qbuf, dcp, dbp, prc, prb, gcs, gbs,
    w_s, w_r, g_s, g_r, z_s, z_r, p_s, p_r, o_s, o_r, x_s, x_r, e_s, e_r, f_s, f_r, h_s, h_r, l_s, l_r, q_s, q_r,
    rc_s, rc_r, ac_s, ac_r, rb_s, rb_r, ab_s, ab_r,
):
    seq = lax.axis_index("seq")
    head = lax.axis_index("head")
    xh = lax.div(seq, 8)
    yy = lax.rem(lax.div(seq, 2), 4)
    core = lax.rem(seq, 2)
    xl = lax.div(head, 8)
    zz = lax.rem(head, 8)
    other = seq + 1 - 2 * core
    beside = (1 - xl) * 8 + zz
    home = lax.rem(zz, 2)
    odd = lax.rem(zz + core, 2)

    own_w = pltpu.make_async_copy(w_hbm, wbuf.at[yy], in_s.at[6])
    own_w.start()
    loads = [
        pltpu.make_async_copy(src, dst, in_s.at[i])
        for i, (src, dst) in enumerate(
            (
                (ld_hbm, ld_ref),
                (dt_hbm, dt_ref),
                (x_hbm, x_ref),
                (b_hbm, b_ref),
                (c_hbm, c_ref),
                (skip_hbm, skip_ref),
            )
        )
    ]
    for load in loads:
        load.start()

    barrier = pltpu.get_barrier_semaphore()

    def greet(s, h):
        pl.semaphore_signal(
            barrier, inc=1, device_id={"seq": s, "head": h}, device_id_type=pl.DeviceIdType.MESH
        )

    over = seq + 8 - 16 * xh
    over_other = other + 8 - 16 * xh
    for h in (beside, head):
        greet(other, h)
        greet(over_other, h)
    greet(over, beside)
    for d in range(1, CHIPS):
        greet(lax.rem(seq + 2 * d, GROUP), head)
    for d in range(1, GROUP):
        greet(seq, lax.rem(head + d, GROUP))
    pl.semaphore_wait(barrier, 5 + CHIPS - 1 + GROUP - 1)

    sent = []

    def start(copy):
        copy.start()
        sent.append(copy)

    go_seq = xl * 8 + yy * 2 + home
    go_slot = gbuf.at[xh * 4 + lax.div(zz, 2), core]
    stays = jnp.logical_and(xl == xh, core == home)
    start(remote(go_hbm, go_slot, g_s.at[0], g_r.at[xh, core], go_seq, beside))
    inside = remote(go_hbm, go_slot, g_s.at[1], g_r.at[xh, core], go_seq, head)
    at_home = pltpu.make_async_copy(go_hbm, go_slot, g_s.at[2])

    @pl.when(jnp.logical_not(stays))
    def _():
        inside.start()

    @pl.when(stays)
    def _():
        at_home.start()

    def hop(name):
        dy, row, way = HOPS[name]
        at = HOP_AT[name]
        where = pl.ds(row, HALF)
        slot = wbuf.at[lax.rem(yy + dy + 4, 4), where]
        src = w_hbm.at[where] if dy == 0 else slot
        to = xh * 8 + lax.rem(yy + (1 if way == "up" else 3), 4) * 2 + core
        return remote(src, slot, w_s.at[at], w_r.at[at], to, head)

    def go(*names):
        for name in names:
            start(hop(name))

    def got(*names):
        for name in names:
            dy, row, way = HOPS[name]
            at = HOP_AT[name]
            dy = dy - 1 if way == "up" else dy + 1
            slot = wbuf.at[lax.rem(yy + dy + 4, 4), pl.ds(row, HALF)]
            remote(slot, slot, w_s.at[at], w_r.at[at], seq, head).wait_recv()

    go("u0", "d1", "u1", "d0")

    def group_at(group):
        return (1 - xh if group == 0 else xh) * 4

    def go_got(group):
        half_at = 1 - xh if group == 0 else xh
        for tok in (1 - core, core):
            slot = gbuf.at[group_at(group) + lax.div(zz, 2), tok]
            came = remote(slot, slot, g_s.at[0], g_r.at[half_at, tok], seq, head)
            if group == 1 and tok is core:

                @pl.when(stays)
                def _():
                    at_home.wait()

                @pl.when(jnp.logical_not(stays))
                def _():
                    came.wait_recv()

            else:
                came.wait_recv()

    def unit(group, way, d, half):
        z_from = lax.rem(zz + (8 - d if way == 0 else d), 8)
        k = group_at(group) + lax.div(z_from, 2)
        return gbuf.at[k, way] if half else gbuf.at[k]

    def z_hop(way, stage, group, is_odd):
        part = unit(group, way, 2 * stage + is_odd, is_odd and stage == 1)
        z_to = lax.rem(zz + (1 if way == 0 else 7), 8)
        return remote(
            part, part, z_s.at[way, stage, group], z_r.at[way, stage, group], seq, xl * 8 + z_to
        )

    def z_got(way, stage, group, is_odd):
        part = unit(group, way, 2 * stage + (1 if is_odd else 2), (not is_odd) and stage == 1)
        remote(
            part, part, z_s.at[way, stage, group], z_r.at[way, stage, group], seq, head
        ).wait_recv()

    def z_pass(stage_in, stage_out, group, is_odd):
        for way in range(2):
            z_got(way, stage_in, group, is_odd)
            if stage_out is not None:
                z_hop(way, stage_out, group, is_odd).start()

    rows_i = lax.broadcasted_iota(jnp.int32, (TOK, TOK), 0)
    cols_i = lax.broadcasted_iota(jnp.int32, (TOK, TOK), 1)
    causal = rows_i >= cols_i
    lower = jnp.where(causal, 1.0, 0.0).astype(F32)
    upper = jnp.where(rows_i <= cols_i, 1.0, 0.0).astype(F32)
    eye = jnp.where(rows_i == cols_i, 1.0, 0.0).astype(F32)
    lane = lax.broadcasted_iota(jnp.int32, (TOK, HEADS), 1)
    lane1 = lax.broadcasted_iota(jnp.int32, (HEADS, 1), 0)
    for load in loads:
        load.wait()
    dt_row = dt_ref[...]
    ld = ld_ref[...]
    run = exact(lower, ld, NT)
    run_row = exact(ld, upper, NN)
    dt = exact(eye, dt_row, NT)
    end = run[TOK - 1 : TOK, :]
    fade = jnp.exp(end - run)
    scale = dt * fade
    rise = jnp.exp(run)
    exp_end = jnp.exp(end)

    @pl.when(odd == 0)
    def _():
        for group in range(2):
            go_got(group)
            for way in range(2):
                z_hop(way, 0, group, 0).start()

    b_all = b_ref[...]
    c_all = c_ref[...]
    for h in range(HEADS):
        ch = slice(h * WIDTH, (h + 1) * WIDTH)
        scaled = x_ref[:, ch].astype(F32) * scale[:, h : h + 1]
        part, rest = split(scaled)
        xs[:, ch] = part
        xs_low[:, ch] = rest
        made = mm(part, b_all, TN) + mm(rest, b_all, TN)
        sfw[2 * h : 2 * h + 2] = made.reshape(2, SLICE, STATE)
        dtile[h] = jnp.broadcast_to(exp_end[:, h : h + 1], (8, 128))

    chip = lax.div(seq, 2)

    def tile(table, q):
        return table[core * (HEADS // 2) + q // 2, 0:1, 0:1]

    def pair_up(own, got_half, pair, first):
        for q in range(CHIPS):
            keep = jnp.where(first, tile(dother, q), 1.0)
            take = jnp.where(first, 1.0, tile(dtile, q))
            pair[q, 0:SLICE] = keep * own[core * CHIPS + q] + take * got_half[q]

    def pair_apart(back, own, got_half, send, out, first):
        for q in range(CHIPS):
            enters = back[q]
            mine = jnp.where(first, 1.0, tile(dother, q))
            here = jnp.where(first, 0.0, 1.0)
            out[core * CHIPS + q] = mine * enters + here * got_half[q]
            theirs = jnp.where(first, tile(dtile, q), 1.0)
            there = jnp.where(first, 1.0, 0.0)
            send[q] = theirs * enters + there * own[core * CHIPS + q]

    def half_of(buf, which):
        return buf.at[pl.ds(pl.multiple_of(which * CHIPS, CHIPS), CHIPS)]

    def to_chips(src, dst, ss, rs):
        for d in range(1, CHIPS):
            peer = lax.rem(chip + d, CHIPS)
            start(remote(src.at[peer], dst.at[chip], ss.at[d], rs.at[d], peer * 2 + core, head))
        dst[chip] = src[chip]

    def from_chips(dst, ss, rs):
        for d in range(1, CHIPS):
            peer = lax.rem(chip + CHIPS - d, CHIPS)
            remote(dst.at[peer], dst.at[peer], ss.at[d], rs.at[d], seq, head).wait_recv()

    first_fw = core == 0
    first_bw = core == 1
    tiles = remote(dtile, dother, e_s.at[0], e_r.at[0], other, head)
    start(tiles)
    halves = remote(half_of(sfw, 1 - core), hin, e_s.at[1], e_r.at[1], other, head)
    start(halves)

    cb[...] = mm(c_all, b_all, NT)
    got("u0")
    go("f0")
    got("d1")
    go("f1")

    tiles.wait_recv()
    halves.wait_recv()
    pair_up(sfw, hin, hpair, first_fw)
    for q in range(CHIPS):
        both = tile(dtile, q) * tile(dother, q)
        hpair[q, SLICE : SLICE + 8] = jnp.broadcast_to(both, (8, STATE))

    @pl.when(odd == 1)
    def _():
        z_pass(0, 0, 0, 1)
        z_pass(0, 0, 1, 1)
        z_pass(1, 1, 0, 1)

    @pl.when(odd == 0)
    def _():
        z_pass(0, 1, 0, 0)
        z_pass(0, 1, 1, 0)
        z_pass(1, None, 0, 0)

    def scan(order, inbox, outbox):
        state = jnp.zeros((SLICE, STATE), F32)
        for q in order:
            outbox[q] = state
            state = state * rfw[q, SLICE : SLICE + 1, :] + inbox[q, 0:SLICE]

    def product(group, acc, n):
        total = None
        for k in range(4):
            left = gbuf[group_at(group) + k].reshape(2 * TOK, COLS)
            new = mm(left, wbuf[k, n * WIDE : (n + 1) * WIDE, :], NT)
            total = new if total is None else total + new
        acc[n] = total.reshape(2, TOK, WIDE)

    own_w.wait()
    got("u1", "d0", "f0", "f1")
    swaps = []
    for n in range(CHUNKS):
        product(0, accp, n)
        swap = remote(accp.at[n, 1 - core], pbufp.at[n], p_s.at[n], p_r.at[n], other, head)
        start(swap)
        swaps.append(swap)
    crossings = []
    for n in range(CHUNKS):
        swaps[n].wait_recv()
        xout[n] = (accp[n, core] + pbufp[n]).astype(BF16)
        cross = remote(xout.at[n], xin.at[n], x_s.at[n], x_r.at[n], over, head)
        start(cross)
        crossings.append(cross)
    to_chips(hpair, rfw, f_s, f_r)

    @pl.when(odd == 1)
    def _():
        z_pass(1, 1, 1, 1)

    @pl.when(odd == 0)
    def _():
        z_pass(1, None, 1, 0)

    swaps = []
    for n in range(CHUNKS):
        product(1, acco, n)
        swap = remote(acco.at[n, 1 - core], pbufo.at[n], o_s.at[n], o_r.at[n], other, head)
        start(swap)
        swaps.append(swap)
    from_chips(rfw, f_s, f_r)
    scan(range(CHIPS), rfw, ofw)
    to_chips(ofw, hback, h_s, h_r)
    for n in range(CHUNKS):
        swaps[n].wait_recv()
        acco[n, core] = acco[n, core] + pbufo[n]

    for h in range(HEADS):
        ch = slice(h * WIDTH, (h + 1) * WIDTH)
        n, at = h // 2, slice((h % 2) * WIDTH, (h % 2 + 1) * WIDTH)
        if h % 2 == 0:
            crossings[n].wait_recv()
        up = (acco[n, core][:, at] + xin[n][:, at].astype(F32)).astype(BF16)
        gy[:, ch] = up
        part, rest = split(up.astype(F32) * rise[:, h : h + 1])
        ge[:, ch] = part
        made = mm(part, c_all, TN) + mm(rest, c_all, TN)
        sbw[2 * h : 2 * h + 2] = made.reshape(2, SLICE, STATE)
    q_halves = remote(half_of(sbw, 1 - core), qin, e_s.at[3], e_r.at[3], other, head)
    start(q_halves)
    q_halves.wait_recv()
    pair_up(sbw, qin, qpair, first_bw)
    to_chips(qpair, rbw, l_s, l_r)
    from_chips(hback, h_s, h_r)
    pair_apart(hback, sfw, hin, hsend, hbuf, first_fw)
    h_swap = remote(hsend, half_of(hbuf, core), e_s.at[2], e_r.at[2], other, head)
    start(h_swap)

    vsum[...] = jnp.zeros((TOK, TOK), F32)
    dcol[...] = jnp.zeros((TOK, HEADS), F32)

    def inner(h):
        ch = slice(h * WIDTH, (h + 1) * WIDTH)
        weights = wts.at[h % 2]
        u_sum = [jnp.zeros((1, WIDTH), F32), jnp.zeros((1, TOK - WIDTH), F32)]
        for r in range(4):
            rows = slice(r * 64, (r + 1) * 64)
            wide = WIDTH if r < 2 else TOK
            gx = mm(gy[rows, ch], x_ref[:wide, ch], NT)
            gaps = run[rows, h : h + 1] - run_row[h : h + 1, :wide]
            decay = jnp.exp(jnp.where(causal[rows, :wide], gaps, -1e30))
            steps = dt_row[h : h + 1, :wide]
            mixed = decay * cb[rows, :wide]
            both = mixed * gx
            vsum[rows, :wide] += decay * gx * steps
            weights[rows, :wide] = (mixed * steps).astype(BF16)
            down = jnp.sum(both, axis=0, keepdims=True)
            u_sum[0] += down[:, :WIDTH]
            if r >= 2:
                u_sum[1] += down[:, WIDTH:]
            along = jnp.sum(both * steps, axis=1, keepdims=True)
            dcol[rows, :] += jnp.where(lane[rows] == h, along, 0.0)
        urow[h : h + 1, :WIDTH] = u_sum[0]
        urow[h : h + 1, WIDTH:] = u_sum[1]
        dxs[:WIDTH, ch] = mm(weights[:, :WIDTH], gy[:, ch], TN)
        dxs[WIDTH:, ch] = mm(weights[WIDTH:, WIDTH:], gy[WIDTH:, ch], TN)

    def inner_read(h):
        ch = slice(h * WIDTH, (h + 1) * WIDTH)
        part, rest = split(hbuf[2 * h : 2 * h + 2].reshape(WIDTH, STATE))
        read = mm(c_all, part, NT) + mm(c_all, rest, NT)
        along = rise[:, h : h + 1] * jnp.sum(gy[:, ch].astype(F32) * read, axis=1, keepdims=True)
        dcol[...] += jnp.where(lane == h, along, 0.0)

    for h in range(HEADS):
        inner(h)
    half = half_of(hbuf, 1 - core)
    remote(half, half, e_s.at[2], e_r.at[2], other, head).wait_recv()

    from_chips(rbw, l_s, l_r)
    scan(range(CHIPS - 1, -1, -1), rbw, obw)
    to_chips(obw, qback, q_s, q_r)

    for h in range(HEADS):
        inner_read(h)
    v_hi = vsum[...].astype(BF16)
    v_lo = (vsum[...] - v_hi.astype(F32)).astype(BF16)

    def spread(src, dst, ss, rs):
        for d in range(1, GROUP):
            peer = lax.rem(head + d, GROUP)
            part = src.at[pl.ds(pl.multiple_of(peer * PART, PART), PART)]
            start(remote(part, dst.at[head], ss.at[d], rs.at[d], seq, peer))
        dst[head] = src[pl.ds(pl.multiple_of(head * PART, PART), PART)]

    def collect(inbox, whole, ss, rs, ss2, rs2):
        for d in range(1, GROUP):
            peer = lax.rem(head + GROUP - d, GROUP)
            remote(inbox.at[peer], inbox.at[peer], ss.at[d], rs.at[d], seq, head).wait_recv()
        total = inbox[0].astype(F32)
        for i in range(1, GROUP):
            total = total + inbox[i].astype(F32)
        own = pl.ds(pl.multiple_of(head * PART, PART), PART)
        whole[own] = total.astype(whole.dtype)
        for d in range(1, GROUP):
            peer = lax.rem(head + d, GROUP)
            start(remote(whole.at[own], whole.at[own], ss2.at[d], rs2.at[d], seq, peer))

    def finish(whole, out, ss, rs):
        for d in range(1, GROUP):
            peer = lax.rem(head + GROUP - d, GROUP)
            part = whole.at[pl.ds(pl.multiple_of(peer * PART, PART), PART)]
            remote(part, part, ss.at[d], rs.at[d], seq, head).wait_recv()
        out[...] = whole[...].astype(F32)

    dcp[...] = (
        mm(v_hi, b_all, NN)
        + mm(v_lo, b_all, NN)
        + mm(ge[...], hbuf[...].reshape(ROWS, STATE).astype(BF16), NN)
    )
    spread(dcp, prc, rc_s, rc_r)
    collect(prc, gcs, rc_s, rc_r, ac_s, ac_r)

    from_chips(qback, q_s, q_r)
    pair_apart(qback, sbw, qin, qsend, qbuf, first_bw)
    q_swap = remote(qsend, half_of(qbuf, core), e_s.at[4], e_r.at[4], other, head)
    start(q_swap)
    half = half_of(qbuf, 1 - core)
    remote(half, half, e_s.at[4], e_r.at[4], other, head).wait_recv()
    part, rest = split(qbuf[...].reshape(ROWS, STATE))
    db = mm(v_hi, c_all, TN) + mm(v_lo, c_all, TN)
    db += mm(xs[...], part, NN) + mm(xs_low[...], part, NN) + mm(xs[...], rest, NN)
    dbp[...] = db.astype(BF16)
    spread(dbp, prb, rb_s, rb_r)

    qcol[...] = jnp.zeros((TOK, HEADS), F32)
    inner_hq = jnp.zeros((HEADS, 1), F32)
    for h in range(HEADS // 2):
        inner_hq = closing(h, lane, lane1, b_all, x_ref, gy, dxs, hbuf, qbuf, qcol, scale, skip_ref, gi_ref, inner_hq)
    collect(prb, gbs, rb_s, rb_r, ab_s, ab_r)
    for h in range(HEADS // 2, HEADS):
        inner_hq = closing(h, lane, lane1, b_all, x_ref, gy, dxs, hbuf, qbuf, qcol, scale, skip_ref, gi_ref, inner_hq)

    step_grad = urow[...] + exact(fade * qcol[...], eye, TN)
    gs_ref[...] = step_grad
    at_end = jnp.sum(exact(scale * qcol[...], eye, TN), axis=1, keepdims=True)
    at_end += jnp.exp(run_row[:, TOK - 1 : TOK]) * inner_hq
    gd_ref[...] = exact(exact(dcol[...], eye, TN) - dt_row * step_grad, lower, NN) + at_end

    finish(gcs, gc_ref, ac_s, ac_r)
    finish(gbs, gb_ref, ab_s, ab_r)

    for copy in sent:
        copy.wait_send()

    @pl.when(jnp.logical_not(stays))
    def _():
        inside.wait_send()

    for is_odd in range(2):

        @pl.when(odd == is_odd)
        def _():
            for stage in range(2):
                for way in range(2):
                    for group in range(2):
                        z_hop(way, stage, group, is_odd).wait_send()


def closing(h, lane, lane1, b_all, x_ref, gy, dxs, hbuf, qbuf, qcol, scale, skip_ref, gi_ref, inner_hq):
    ch = slice(h * WIDTH, (h + 1) * WIDTH)
    grad = qbuf[2 * h : 2 * h + 2].reshape(WIDTH, STATE)
    part, rest = split(grad)
    fed = mm(b_all, part, NT) + mm(b_all, rest, NT)
    met = jnp.sum(x_ref[:, ch].astype(F32) * fed, axis=1, keepdims=True)
    qcol[...] += jnp.where(lane == h, met, 0.0)
    gi_ref[:, ch] = (
        dxs[:, ch]
        + skip_ref[:, h : h + 1] * gy[:, ch].astype(F32)
        + scale[:, h : h + 1] * fed
    ).astype(BF16)
    state = hbuf[2 * h : 2 * h + 2].reshape(WIDTH, STATE)
    prod = state * grad
    total = jnp.sum(jnp.sum(prod, axis=0, keepdims=True), axis=1, keepdims=True)
    return inner_hq + jnp.where(lane1 == h, total, 0.0)


def hand_over(*refs):
    given, out, room, sems = refs[:5], refs[5:10], refs[10:15], refs[15]
    come = [pltpu.make_async_copy(given[i], room[i], sems.at[i]) for i in range(5)]
    leave = [pltpu.make_async_copy(room[i], out[i], sems.at[5 + i]) for i in range(5)]
    for copy in come:
        copy.start()
    for i in range(5):
        come[i].wait()
        leave[i].start()
    for copy in leave:
        copy.wait()


def local(grad_out, out_weight, ssm_input, step_size, log_decay, b_in, c_in, skip):
    vmem = pl.BlockSpec(memory_space=pltpu.VMEM)
    here = pl.BlockSpec(memory_space=pl.ANY)
    dma = pltpu.SemaphoreType.DMA
    slices = pltpu.VMEM((GROUP, SLICE, STATE), F32)
    halves = pltpu.VMEM((CHIPS, SLICE, STATE), F32)
    tagged = pltpu.VMEM((CHIPS, SLICE + 8, STATE), F32)
    parts = pltpu.VMEM((GROUP, PART, STATE), F32)
    short_parts = pltpu.VMEM((GROUP, PART, STATE), BF16)
    short_square = pltpu.VMEM((TOK, STATE), BF16)
    square = pltpu.VMEM((TOK, STATE), F32)
    by_row = pltpu.VMEM((HEADS, TOK), F32)
    sums = pltpu.VMEM((CHUNKS, TOK, WIDE), F32)
    short = pltpu.VMEM((CHUNKS, TOK, WIDE), BF16)
    by_head = pltpu.VMEM((TOK, HEADS), F32)
    wide = pltpu.VMEM((TOK, ROWS), BF16)
    peers = dma((GROUP,))
    gi, gs, gd, gb, gc = pl.pallas_call(
        kernel,
        out_shape=(
            jax.ShapeDtypeStruct((TOK, ROWS), BF16),
            jax.ShapeDtypeStruct((HEADS, TOK), F32),
            jax.ShapeDtypeStruct((HEADS, TOK), F32),
            jax.ShapeDtypeStruct((TOK, STATE), F32),
            jax.ShapeDtypeStruct((TOK, STATE), F32),
        ),
        in_specs=[here] * 8,
        out_specs=[vmem] * 5,
        scratch_shapes=[
            wide,
            by_row, by_row,
            pltpu.VMEM((TOK, STATE), BF16), pltpu.VMEM((TOK, STATE), BF16),
            pltpu.VMEM((1, HEADS), F32),
            dma((7,)),
            pltpu.VMEM((4, ROWS, COLS), BF16),
            pltpu.VMEM((8, 2, TOK, COLS), BF16),
            pltpu.VMEM((CHUNKS, 2, TOK, WIDE), F32), pltpu.VMEM((CHUNKS, 2, TOK, WIDE), F32),
            sums, sums, short, short,
            wide,
            wide,
            wide, wide,
            pltpu.VMEM((2, TOK, TOK), BF16),
            pltpu.VMEM((TOK, ROWS), F32),
            pltpu.VMEM((TOK, TOK), F32),
            pltpu.VMEM((TOK, TOK), F32),
            pltpu.VMEM((HEADS, TOK), F32),
            by_head,
            by_head,
            pltpu.VMEM((HEADS, 8, 128), F32),
            pltpu.VMEM((HEADS, 8, 128), F32),
            slices, halves, tagged, tagged, halves, halves, halves, slices,
            slices, halves, halves, halves, halves, halves, halves, slices,
            square, short_square,
            parts, short_parts,
            square, short_square,
            dma((len(HOPS),)), dma((len(HOPS),)),
            dma((3,)), dma((2, 2)),
            dma((2, 2, 2)), dma((2, 2, 2)),
            dma((CHUNKS,)), dma((CHUNKS,)),
            dma((CHUNKS,)), dma((CHUNKS,)),
            dma((CHUNKS,)), dma((CHUNKS,)),
        ] + [peers] * 18,
        compiler_params=pltpu.CompilerParams(
            collective_id=0, has_side_effects=True, vmem_limit_bytes=60 * 2**20
        ),
        name="layer_backward",
    )(
        grad_out, out_weight, ssm_input, step_size.T, log_decay.T, b_in, c_in, skip.reshape(1, HEADS)
    )
    gi, gs, gd, gb, gc = pl.pallas_call(
        hand_over,
        out_shape=tuple(jax.ShapeDtypeStruct(a.shape, a.dtype) for a in (gi, gs, gd, gb, gc)),
        in_specs=[here] * 5,
        out_specs=[here] * 5,
        scratch_shapes=[pltpu.VMEM(a.shape, a.dtype) for a in (gi, gs, gd, gb, gc)] + [dma((10,))],
        name="hand_over",
    )(gi, gs, gd, gb, gc)
    return gi, gs.T, gd.T, gb, gc


def solution(mesh):
    in_specs = (
        P("seq", "head"),
        P("head", "seq"),
        P("seq", "head"),
        P("seq", "head"),
        P("seq", "head"),
        P("seq", None),
        P("seq", None),
        P("head"),
    )
    out_specs = (
        P("seq", "head"),
        P("seq", "head"),
        P("seq", "head"),
        P("seq", None),
        P("seq", None),
    )
    return jax.shard_map(local, mesh=mesh, in_specs=in_specs, out_specs=out_specs, check_vma=False)
```

```python
import jax
import jax.numpy as jnp
from jax import lax
from jax.experimental import pallas as pl
from jax.experimental.pallas import tpu as pltpu
from jax.sharding import PartitionSpec as P

F32, BF16 = jnp.float32, jnp.bfloat16
HIGH = lax.Precision.HIGHEST
NN = (((1,), (0,)), ((), ()))
NT = (((1,), (1,)), ((), ()))
TN = (((0,), (0,)), ((), ()))

TOK = 256
HEADS = 8
WIDTH = 128
STATE = 256
ROWS = HEADS * WIDTH
COLS = 512
GROUP = 16
CHIPS = 8
SLICE = ROWS // GROUP
PART = TOK // GROUP
HALF = ROWS // 2
CHUNKS = 4
WIDE = ROWS // CHUNKS


def mm(a, b, dims):
    return lax.dot_general(a, b, dims, preferred_element_type=F32)


def exact(a, b, dims):
    return lax.dot_general(a, b, dims, precision=HIGH, preferred_element_type=F32)


def split(a):
    high = a.astype(BF16)
    return high, (a - high.astype(F32)).astype(BF16)


def remote(src, dst, send_sem, recv_sem, seq, head):
    return pltpu.make_async_remote_copy(
        src_ref=src,
        dst_ref=dst,
        send_sem=send_sem,
        recv_sem=recv_sem,
        device_id={"seq": seq, "head": head},
        device_id_type=pl.DeviceIdType.MESH,
    )


HOPS = {
    "u0": (0, 0, "up"),
    "d1": (0, HALF, "down"),
    "u1": (0, HALF, "up"),
    "d0": (0, 0, "down"),
    "f0": (-1, 0, "up"),
    "f1": (1, HALF, "down"),
}
HOP_AT = {name: at for at, name in enumerate(HOPS)}


def kernel(
    go_hbm, w_hbm, x_hbm, dt_hbm, ld_hbm, b_hbm, c_hbm, skip_hbm,
    gi_ref, gs_ref, gd_ref, gb_ref, gc_ref,
    x_ref, dt_ref, ld_ref, b_ref, c_ref, skip_ref, in_s,
    wbuf, gbuf, accp, acco, pbufp, pbufo, xout, xin, gy, ge, ge_low, xs, xs_low, wts, dxs, cb, vsum, urow, dcol, qcol, dtile, dother,
    sfw, hin, hpair, rfw, ofw, hback, hsend, hbuf,
    sbw, qin, qpair, rbw, obw, qback, qsend, qbuf, dcp, dbp, prc, prb, gcs, gbs,
    w_s, w_r, g_s, g_r, z_s, z_r, p_s, p_r, o_s, o_r, x_s, x_r, e_s, e_r, f_s, f_r, h_s, h_r, l_s, l_r, q_s, q_r,
    rc_s, rc_r, ac_s, ac_r, rb_s, rb_r, ab_s, ab_r,
):
    seq = lax.axis_index("seq")
    head = lax.axis_index("head")
    xh = lax.div(seq, 8)
    yy = lax.rem(lax.div(seq, 2), 4)
    core = lax.rem(seq, 2)
    xl = lax.div(head, 8)
    zz = lax.rem(head, 8)
    other = seq + 1 - 2 * core
    beside = (1 - xl) * 8 + zz
    home = lax.rem(zz, 2)
    odd = lax.rem(zz + core, 2)

    own_w = pltpu.make_async_copy(w_hbm, wbuf.at[yy], in_s.at[6])
    own_w.start()
    loads = [
        pltpu.make_async_copy(src, dst, in_s.at[i])
        for i, (src, dst) in enumerate(
            (
                (ld_hbm, ld_ref),
                (dt_hbm, dt_ref),
                (x_hbm, x_ref),
                (b_hbm, b_ref),
                (c_hbm, c_ref),
                (skip_hbm, skip_ref),
            )
        )
    ]
    for load in loads:
        load.start()

    barrier = pltpu.get_barrier_semaphore()

    def greet(s, h):
        pl.semaphore_signal(
            barrier, inc=1, device_id={"seq": s, "head": h}, device_id_type=pl.DeviceIdType.MESH
        )

    over = seq + 8 - 16 * xh
    over_other = other + 8 - 16 * xh
    for h in (beside, head):
        greet(other, h)
        greet(over_other, h)
    greet(over, beside)
    for d in range(1, CHIPS):
        greet(lax.rem(seq + 2 * d, GROUP), head)
    for d in range(1, GROUP):
        greet(seq, lax.rem(head + d, GROUP))
    pl.semaphore_wait(barrier, 5 + CHIPS - 1 + GROUP - 1)

    sent = []

    def start(copy):
        copy.start()
        sent.append(copy)

    go_seq = xl * 8 + yy * 2 + home
    go_slot = gbuf.at[xh * 4 + lax.div(zz, 2), core]
    stays = jnp.logical_and(xl == xh, core == home)
    start(remote(go_hbm, go_slot, g_s.at[0], g_r.at[xh, core], go_seq, beside))
    inside = remote(go_hbm, go_slot, g_s.at[1], g_r.at[xh, core], go_seq, head)
    at_home = pltpu.make_async_copy(go_hbm, go_slot, g_s.at[2])

    @pl.when(jnp.logical_not(stays))
    def _():
        inside.start()

    @pl.when(stays)
    def _():
        at_home.start()

    def hop(name):
        dy, row, way = HOPS[name]
        at = HOP_AT[name]
        where = pl.ds(row, HALF)
        slot = wbuf.at[lax.rem(yy + dy + 4, 4), where]
        src = w_hbm.at[where] if dy == 0 else slot
        to = xh * 8 + lax.rem(yy + (1 if way == "up" else 3), 4) * 2 + core
        return remote(src, slot, w_s.at[at], w_r.at[at], to, head)

    def go(*names):
        for name in names:
            start(hop(name))

    def got(*names):
        for name in names:
            dy, row, way = HOPS[name]
            at = HOP_AT[name]
            dy = dy - 1 if way == "up" else dy + 1
            slot = wbuf.at[lax.rem(yy + dy + 4, 4), pl.ds(row, HALF)]
            remote(slot, slot, w_s.at[at], w_r.at[at], seq, head).wait_recv()

    go("u0", "d1", "u1", "d0")

    def group_at(group):
        return (1 - xh if group == 0 else xh) * 4

    def go_got(group):
        half_at = 1 - xh if group == 0 else xh
        for tok in (1 - core, core):
            slot = gbuf.at[group_at(group) + lax.div(zz, 2), tok]
            came = remote(slot, slot, g_s.at[0], g_r.at[half_at, tok], seq, head)
            if group == 1 and tok is core:

                @pl.when(stays)
                def _():
                    at_home.wait()

                @pl.when(jnp.logical_not(stays))
                def _():
                    came.wait_recv()

            else:
                came.wait_recv()

    def unit(group, way, d, half):
        z_from = lax.rem(zz + (8 - d if way == 0 else d), 8)
        k = group_at(group) + lax.div(z_from, 2)
        return gbuf.at[k, way] if half else gbuf.at[k]

    def z_hop(way, stage, group, is_odd):
        part = unit(group, way, 2 * stage + is_odd, is_odd and stage == 1)
        z_to = lax.rem(zz + (1 if way == 0 else 7), 8)
        return remote(
            part, part, z_s.at[way, stage, group], z_r.at[way, stage, group], seq, xl * 8 + z_to
        )

    def z_got(way, stage, group, is_odd):
        part = unit(group, way, 2 * stage + (1 if is_odd else 2), (not is_odd) and stage == 1)
        remote(
            part, part, z_s.at[way, stage, group], z_r.at[way, stage, group], seq, head
        ).wait_recv()

    def z_pass(stage_in, stage_out, group, is_odd):
        for way in range(2):
            z_got(way, stage_in, group, is_odd)
            if stage_out is not None:
                z_hop(way, stage_out, group, is_odd).start()

    rows_i = lax.broadcasted_iota(jnp.int32, (TOK, TOK), 0)
    cols_i = lax.broadcasted_iota(jnp.int32, (TOK, TOK), 1)
    causal = rows_i >= cols_i
    lower = jnp.where(causal, 1.0, 0.0).astype(F32)
    upper = jnp.where(rows_i <= cols_i, 1.0, 0.0).astype(F32)
    eye = jnp.where(rows_i == cols_i, 1.0, 0.0).astype(F32)
    lane = lax.broadcasted_iota(jnp.int32, (TOK, HEADS), 1)
    lane1 = lax.broadcasted_iota(jnp.int32, (HEADS, 1), 0)
    for load in loads:
        load.wait()
    dt_row = dt_ref[...]
    ld = ld_ref[...]
    run = exact(lower, ld, NT)
    run_row = exact(ld, upper, NN)
    dt = exact(eye, dt_row, NT)
    end = run[TOK - 1 : TOK, :]
    fade = jnp.exp(end - run)
    scale = dt * fade
    rise = jnp.exp(run)
    exp_end = jnp.exp(end)

    def z_begin(group):
        go_got(group)
        for way in range(2):
            z_hop(way, 0, group, 0).start()

    @pl.when(odd == 0)
    def _():
        z_begin(0)

    b_all = b_ref[...]
    c_all = c_ref[...]
    for h in range(HEADS):
        ch = slice(h * WIDTH, (h + 1) * WIDTH)
        scaled = x_ref[:, ch].astype(F32) * scale[:, h : h + 1]
        part, rest = split(scaled)
        xs[:, ch] = part
        xs_low[:, ch] = rest
        made = mm(part, b_all, TN) + mm(rest, b_all, TN)
        sfw[2 * h : 2 * h + 2] = made.reshape(2, SLICE, STATE)
        dtile[h] = jnp.broadcast_to(exp_end[:, h : h + 1], (8, 128))

    chip = lax.div(seq, 2)

    def tile(table, q):
        return table[core * (HEADS // 2) + q // 2, 0:1, 0:1]

    def pair_up(own, got_half, pair, first):
        for q in range(CHIPS):
            keep = jnp.where(first, tile(dother, q), 1.0)
            take = jnp.where(first, 1.0, tile(dtile, q))
            pair[q, 0:SLICE] = keep * own[core * CHIPS + q] + take * got_half[q]

    def pair_apart(back, own, got_half, send, out, first):
        for q in range(CHIPS):
            enters = back[q]
            mine = jnp.where(first, 1.0, tile(dother, q))
            here = jnp.where(first, 0.0, 1.0)
            out[core * CHIPS + q] = mine * enters + here * got_half[q]
            theirs = jnp.where(first, tile(dtile, q), 1.0)
            there = jnp.where(first, 1.0, 0.0)
            send[q] = theirs * enters + there * own[core * CHIPS + q]

    def half_of(buf, which):
        return buf.at[pl.ds(pl.multiple_of(which * CHIPS, CHIPS), CHIPS)]

    def to_chips(src, dst, ss, rs):
        for d in range(1, CHIPS):
            peer = lax.rem(chip + d, CHIPS)
            start(remote(src.at[peer], dst.at[chip], ss.at[d], rs.at[d], peer * 2 + core, head))
        dst[chip] = src[chip]

    def from_chips(dst, ss, rs):
        for d in range(1, CHIPS):
            peer = lax.rem(chip + CHIPS - d, CHIPS)
            remote(dst.at[peer], dst.at[peer], ss.at[d], rs.at[d], seq, head).wait_recv()

    first_fw = core == 0
    first_bw = core == 1
    tiles = remote(dtile, dother, e_s.at[0], e_r.at[0], other, head)
    start(tiles)
    halves = remote(half_of(sfw, 1 - core), hin, e_s.at[1], e_r.at[1], other, head)
    start(halves)

    cb[...] = mm(c_all, b_all, NT)
    got("u0")
    go("f0")
    got("d1")
    go("f1")

    @pl.when(odd == 1)
    def _():
        z_pass(0, 0, 0, 1)

    tiles.wait_recv()
    halves.wait_recv()
    pair_up(sfw, hin, hpair, first_fw)
    for q in range(CHIPS):
        both = tile(dtile, q) * tile(dother, q)
        hpair[q, SLICE : SLICE + 8] = jnp.broadcast_to(both, (8, STATE))

    @pl.when(odd == 0)
    def _():
        z_pass(0, 1, 0, 0)
        z_begin(1)

    @pl.when(odd == 1)
    def _():
        z_pass(1, 1, 0, 1)
        z_pass(0, 0, 1, 1)

    @pl.when(odd == 0)
    def _():
        z_pass(1, None, 0, 0)
        z_pass(0, 1, 1, 0)

    def scan(order, inbox, outbox):
        state = jnp.zeros((SLICE, STATE), F32)
        for q in order:
            outbox[q] = state
            state = state * rfw[q, SLICE : SLICE + 1, :] + inbox[q, 0:SLICE]

    def product(group, acc, n):
        total = None
        for k in range(4):
            left = gbuf[group_at(group) + k].reshape(2 * TOK, COLS)
            new = mm(left, wbuf[k, n * WIDE : (n + 1) * WIDE, :], NT)
            total = new if total is None else total + new
        acc[n] = total.reshape(2, TOK, WIDE)

    own_w.wait()
    got("u1", "d0", "f0", "f1")
    crossings = []

    def cross_over(n):
        swaps[n].wait_recv()
        xout[n] = (accp[n, core] + pbufp[n]).astype(BF16)
        cross = remote(xout.at[n], xin.at[n], x_s.at[n], x_r.at[n], over, head)
        start(cross)
        crossings.append(cross)

    swaps = []
    for n in range(CHUNKS):
        product(0, accp, n)
        swap = remote(accp.at[n, 1 - core], pbufp.at[n], p_s.at[n], p_r.at[n], other, head)
        start(swap)
        swaps.append(swap)
        if n > 0:
            cross_over(n - 1)
    cross_over(CHUNKS - 1)
    to_chips(hpair, rfw, f_s, f_r)

    @pl.when(odd == 1)
    def _():
        z_pass(1, 1, 1, 1)

    @pl.when(odd == 0)
    def _():
        z_pass(1, None, 1, 0)

    swaps = []
    for n in range(CHUNKS):
        product(1, acco, n)
        swap = remote(acco.at[n, 1 - core], pbufo.at[n], o_s.at[n], o_r.at[n], other, head)
        start(swap)
        swaps.append(swap)
    from_chips(rfw, f_s, f_r)
    scan(range(CHIPS), rfw, ofw)
    to_chips(ofw, hback, h_s, h_r)
    for n in range(CHUNKS):
        swaps[n].wait_recv()
        acco[n, core] = acco[n, core] + pbufo[n]

    for h in range(HEADS):
        ch = slice(h * WIDTH, (h + 1) * WIDTH)
        n, at = h // 2, slice((h % 2) * WIDTH, (h % 2 + 1) * WIDTH)
        if h % 2 == 0:
            crossings[n].wait_recv()
        up = (acco[n, core][:, at] + xin[n][:, at].astype(F32)).astype(BF16)
        gy[:, ch] = up
        part, rest = split(up.astype(F32) * rise[:, h : h + 1])
        ge[:, ch] = part
        ge_low[:, ch] = rest
        made = mm(part, c_all, TN) + mm(rest, c_all, TN)
        sbw[2 * h : 2 * h + 2] = made.reshape(2, SLICE, STATE)
    q_halves = remote(half_of(sbw, 1 - core), qin, e_s.at[3], e_r.at[3], other, head)
    start(q_halves)
    q_halves.wait_recv()
    pair_up(sbw, qin, qpair, first_bw)
    to_chips(qpair, rbw, l_s, l_r)
    from_chips(hback, h_s, h_r)
    pair_apart(hback, sfw, hin, hsend, hbuf, first_fw)
    h_swap = remote(hsend, half_of(hbuf, core), e_s.at[2], e_r.at[2], other, head)
    start(h_swap)

    vsum[...] = jnp.zeros((TOK, TOK), F32)
    dcol[...] = jnp.zeros((TOK, HEADS), F32)

    def inner(h):
        ch = slice(h * WIDTH, (h + 1) * WIDTH)
        weights = wts.at[h % 2]
        u_sum = [jnp.zeros((1, WIDTH), F32), jnp.zeros((1, TOK - WIDTH), F32)]
        for r in range(4):
            rows = slice(r * 64, (r + 1) * 64)
            wide = WIDTH if r < 2 else TOK
            gx = mm(gy[rows, ch], x_ref[:wide, ch], NT)
            gaps = run[rows, h : h + 1] - run_row[h : h + 1, :wide]
            decay = jnp.exp(jnp.where(causal[rows, :wide], gaps, -1e30))
            steps = dt_row[h : h + 1, :wide]
            mixed = decay * cb[rows, :wide]
            both = mixed * gx
            vsum[rows, :wide] += decay * gx * steps
            weights[rows, :wide] = (mixed * steps).astype(BF16)
            down = jnp.sum(both, axis=0, keepdims=True)
            u_sum[0] += down[:, :WIDTH]
            if r >= 2:
                u_sum[1] += down[:, WIDTH:]
            along = jnp.sum(both * steps, axis=1, keepdims=True)
            dcol[rows, :] += jnp.where(lane[rows] == h, along, 0.0)
        urow[h : h + 1, :WIDTH] = u_sum[0]
        urow[h : h + 1, WIDTH:] = u_sum[1]
        dxs[:WIDTH, ch] = mm(weights[:, :WIDTH], gy[:, ch], TN)
        dxs[WIDTH:, ch] = mm(weights[WIDTH:, WIDTH:], gy[WIDTH:, ch], TN)

    def inner_read(h):
        ch = slice(h * WIDTH, (h + 1) * WIDTH)
        part, rest = split(hbuf[2 * h : 2 * h + 2].reshape(WIDTH, STATE))
        read = mm(c_all, part, NT) + mm(c_all, rest, NT)
        along = rise[:, h : h + 1] * jnp.sum(gy[:, ch].astype(F32) * read, axis=1, keepdims=True)
        dcol[...] += jnp.where(lane == h, along, 0.0)

    for h in range(HEADS):
        inner(h)
    half = half_of(hbuf, 1 - core)
    remote(half, half, e_s.at[2], e_r.at[2], other, head).wait_recv()

    from_chips(rbw, l_s, l_r)
    scan(range(CHIPS - 1, -1, -1), rbw, obw)
    to_chips(obw, qback, q_s, q_r)

    for h in range(HEADS):
        inner_read(h)
    v_hi = vsum[...].astype(BF16)
    v_lo = (vsum[...] - v_hi.astype(F32)).astype(BF16)

    def spread(src, dst, ss, rs):
        for d in range(1, GROUP):
            peer = lax.rem(head + d, GROUP)
            part = src.at[pl.ds(pl.multiple_of(peer * PART, PART), PART)]
            start(remote(part, dst.at[head], ss.at[d], rs.at[d], seq, peer))
        dst[head] = src[pl.ds(pl.multiple_of(head * PART, PART), PART)]

    def collect(inbox, whole, ss, rs, ss2, rs2):
        for d in range(1, GROUP):
            peer = lax.rem(head + GROUP - d, GROUP)
            remote(inbox.at[peer], inbox.at[peer], ss.at[d], rs.at[d], seq, head).wait_recv()
        total = inbox[0].astype(F32)
        for i in range(1, GROUP):
            total = total + inbox[i].astype(F32)
        own = pl.ds(pl.multiple_of(head * PART, PART), PART)
        whole[own] = total.astype(whole.dtype)
        for d in range(1, GROUP):
            peer = lax.rem(head + d, GROUP)
            start(remote(whole.at[own], whole.at[own], ss2.at[d], rs2.at[d], seq, peer))

    def finish(whole, out, ss, rs):
        for d in range(1, GROUP):
            peer = lax.rem(head + GROUP - d, GROUP)
            part = whole.at[pl.ds(pl.multiple_of(peer * PART, PART), PART)]
            remote(part, part, ss.at[d], rs.at[d], seq, head).wait_recv()
        out[...] = whole[...].astype(F32)

    part, rest = split(hbuf[...].reshape(ROWS, STATE))
    dc = mm(v_hi, b_all, NN) + mm(v_lo, b_all, NN)
    dc += mm(ge[...], part, NN) + mm(ge_low[...], part, NN) + mm(ge[...], rest, NN)
    dcp[...] = dc.astype(BF16)
    spread(dcp, prc, rc_s, rc_r)

    from_chips(qback, q_s, q_r)
    pair_apart(qback, sbw, qin, qsend, qbuf, first_bw)
    q_swap = remote(qsend, half_of(qbuf, core), e_s.at[4], e_r.at[4], other, head)
    start(q_swap)
    half = half_of(qbuf, 1 - core)
    remote(half, half, e_s.at[4], e_r.at[4], other, head).wait_recv()
    part, rest = split(qbuf[...].reshape(ROWS, STATE))
    db = mm(v_hi, c_all, TN) + mm(v_lo, c_all, TN)
    db += mm(xs[...], part, NN) + mm(xs_low[...], part, NN) + mm(xs[...], rest, NN)
    dbp[...] = db.astype(BF16)
    spread(dbp, prb, rb_s, rb_r)
    collect(prc, gcs, rc_s, rc_r, ac_s, ac_r)

    qcol[...] = jnp.zeros((TOK, HEADS), F32)
    inner_hq = jnp.zeros((HEADS, 1), F32)
    for h in range(HEADS // 2):
        inner_hq = closing(h, lane, lane1, b_all, x_ref, gy, dxs, hbuf, qbuf, qcol, scale, skip_ref, gi_ref, inner_hq)
    collect(prb, gbs, rb_s, rb_r, ab_s, ab_r)
    for h in range(HEADS // 2, HEADS):
        inner_hq = closing(h, lane, lane1, b_all, x_ref, gy, dxs, hbuf, qbuf, qcol, scale, skip_ref, gi_ref, inner_hq)

    step_grad = urow[...] + exact(fade * qcol[...], eye, TN)
    gs_ref[...] = step_grad
    at_end = jnp.sum(exact(scale * qcol[...], eye, TN), axis=1, keepdims=True)
    at_end += jnp.exp(run_row[:, TOK - 1 : TOK]) * inner_hq
    gd_ref[...] = exact(exact(dcol[...], eye, TN) - dt_row * step_grad, lower, NN) + at_end

    finish(gcs, gc_ref, ac_s, ac_r)
    finish(gbs, gb_ref, ab_s, ab_r)

    for copy in sent:
        copy.wait_send()

    @pl.when(jnp.logical_not(stays))
    def _():
        inside.wait_send()

    for is_odd in range(2):

        @pl.when(odd == is_odd)
        def _():
            for stage in range(2):
                for way in range(2):
                    for group in range(2):
                        z_hop(way, stage, group, is_odd).wait_send()


def closing(h, lane, lane1, b_all, x_ref, gy, dxs, hbuf, qbuf, qcol, scale, skip_ref, gi_ref, inner_hq):
    ch = slice(h * WIDTH, (h + 1) * WIDTH)
    grad = qbuf[2 * h : 2 * h + 2].reshape(WIDTH, STATE)
    part, rest = split(grad)
    fed = mm(b_all, part, NT) + mm(b_all, rest, NT)
    met = jnp.sum(x_ref[:, ch].astype(F32) * fed, axis=1, keepdims=True)
    qcol[...] += jnp.where(lane == h, met, 0.0)
    gi_ref[:, ch] = (
        dxs[:, ch]
        + skip_ref[:, h : h + 1] * gy[:, ch].astype(F32)
        + scale[:, h : h + 1] * fed
    ).astype(BF16)
    state = hbuf[2 * h : 2 * h + 2].reshape(WIDTH, STATE)
    prod = state * grad
    total = jnp.sum(jnp.sum(prod, axis=0, keepdims=True), axis=1, keepdims=True)
    return inner_hq + jnp.where(lane1 == h, total, 0.0)


def hand_over(*refs):
    given, out, room, sems = refs[:5], refs[5:10], refs[10:15], refs[15]
    come = [pltpu.make_async_copy(given[i], room[i], sems.at[i]) for i in range(5)]
    leave = [pltpu.make_async_copy(room[i], out[i], sems.at[5 + i]) for i in range(5)]
    for copy in come:
        copy.start()
    for i in range(5):
        come[i].wait()
        leave[i].start()
    for copy in leave:
        copy.wait()


def local(grad_out, out_weight, ssm_input, step_size, log_decay, b_in, c_in, skip):
    vmem = pl.BlockSpec(memory_space=pltpu.VMEM)
    here = pl.BlockSpec(memory_space=pl.ANY)
    dma = pltpu.SemaphoreType.DMA
    slices = pltpu.VMEM((GROUP, SLICE, STATE), F32)
    halves = pltpu.VMEM((CHIPS, SLICE, STATE), F32)
    tagged = pltpu.VMEM((CHIPS, SLICE + 8, STATE), F32)
    short_parts = pltpu.VMEM((GROUP, PART, STATE), BF16)
    short_square = pltpu.VMEM((TOK, STATE), BF16)
    by_row = pltpu.VMEM((HEADS, TOK), F32)
    sums = pltpu.VMEM((CHUNKS, TOK, WIDE), F32)
    short = pltpu.VMEM((CHUNKS, TOK, WIDE), BF16)
    by_head = pltpu.VMEM((TOK, HEADS), F32)
    wide = pltpu.VMEM((TOK, ROWS), BF16)
    peers = dma((GROUP,))
    gi, gs, gd, gb, gc = pl.pallas_call(
        kernel,
        out_shape=(
            jax.ShapeDtypeStruct((TOK, ROWS), BF16),
            jax.ShapeDtypeStruct((HEADS, TOK), F32),
            jax.ShapeDtypeStruct((HEADS, TOK), F32),
            jax.ShapeDtypeStruct((TOK, STATE), F32),
            jax.ShapeDtypeStruct((TOK, STATE), F32),
        ),
        in_specs=[here] * 8,
        out_specs=[vmem] * 5,
        scratch_shapes=[
            wide,
            by_row, by_row,
            pltpu.VMEM((TOK, STATE), BF16), pltpu.VMEM((TOK, STATE), BF16),
            pltpu.VMEM((1, HEADS), F32),
            dma((7,)),
            pltpu.VMEM((4, ROWS, COLS), BF16),
            pltpu.VMEM((8, 2, TOK, COLS), BF16),
            pltpu.VMEM((CHUNKS, 2, TOK, WIDE), F32), pltpu.VMEM((CHUNKS, 2, TOK, WIDE), F32),
            sums, sums, short, short,
            wide,
            wide, wide,
            wide, wide,
            pltpu.VMEM((2, TOK, TOK), BF16),
            pltpu.VMEM((TOK, ROWS), F32),
            pltpu.VMEM((TOK, TOK), F32),
            pltpu.VMEM((TOK, TOK), F32),
            pltpu.VMEM((HEADS, TOK), F32),
            by_head,
            by_head,
            pltpu.VMEM((HEADS, 8, 128), F32),
            pltpu.VMEM((HEADS, 8, 128), F32),
            slices, halves, tagged, tagged, halves, halves, halves, slices,
            slices, halves, halves, halves, halves, halves, halves, slices,
            short_square, short_square,
            short_parts, short_parts,
            short_square, short_square,
            dma((len(HOPS),)), dma((len(HOPS),)),
            dma((3,)), dma((2, 2)),
            dma((2, 2, 2)), dma((2, 2, 2)),
            dma((CHUNKS,)), dma((CHUNKS,)),
            dma((CHUNKS,)), dma((CHUNKS,)),
            dma((CHUNKS,)), dma((CHUNKS,)),
        ] + [peers] * 18,
        compiler_params=pltpu.CompilerParams(
            collective_id=0, has_side_effects=True, vmem_limit_bytes=60 * 2**20
        ),
        name="layer_backward",
    )(
        grad_out, out_weight, ssm_input, step_size.T, log_decay.T, b_in, c_in, skip.reshape(1, HEADS)
    )
    gi, gs, gd, gb, gc = pl.pallas_call(
        hand_over,
        out_shape=tuple(jax.ShapeDtypeStruct(a.shape, a.dtype) for a in (gi, gs, gd, gb, gc)),
        in_specs=[here] * 5,
        out_specs=[here] * 5,
        scratch_shapes=[pltpu.VMEM(a.shape, a.dtype) for a in (gi, gs, gd, gb, gc)] + [dma((10,))],
        name="hand_over",
    )(gi, gs, gd, gb, gc)
    return gi, gs.T, gd.T, gb, gc


def solution(mesh):
    in_specs = (
        P("seq", "head"),
        P("head", "seq"),
        P("seq", "head"),
        P("seq", "head"),
        P("seq", "head"),
        P("seq", None),
        P("seq", None),
        P("head"),
    )
    out_specs = (
        P("seq", "head"),
        P("seq", "head"),
        P("seq", "head"),
        P("seq", None),
        P("seq", None),
    )
    return jax.shard_map(local, mesh=mesh, in_specs=in_specs, out_specs=out_specs, check_vma=False)
```

```python
import jax
import jax.numpy as jnp
from jax import lax
from jax.experimental import pallas as pl
from jax.experimental.pallas import tpu as pltpu
from jax.sharding import PartitionSpec as P

F32, BF16 = jnp.float32, jnp.bfloat16
HIGH = lax.Precision.HIGHEST
NN = (((1,), (0,)), ((), ()))
NT = (((1,), (1,)), ((), ()))
TN = (((0,), (0,)), ((), ()))

TOK = 256
HEADS = 8
WIDTH = 128
STATE = 256
ROWS = HEADS * WIDTH
COLS = 512
GROUP = 16
CHIPS = 8
SLICE = ROWS // GROUP
PART = TOK // GROUP
HALF = ROWS // 2
CHUNKS = 4
WIDE = ROWS // CHUNKS


def mm(a, b, dims):
    return lax.dot_general(a, b, dims, preferred_element_type=F32)


def exact(a, b, dims):
    return lax.dot_general(a, b, dims, precision=HIGH, preferred_element_type=F32)


def split(a):
    high = a.astype(BF16)
    return high, (a - high.astype(F32)).astype(BF16)


def remote(src, dst, send_sem, recv_sem, seq, head):
    return pltpu.make_async_remote_copy(
        src_ref=src,
        dst_ref=dst,
        send_sem=send_sem,
        recv_sem=recv_sem,
        device_id={"seq": seq, "head": head},
        device_id_type=pl.DeviceIdType.MESH,
    )


HOPS = {
    "u0": (0, 0, "up"),
    "d1": (0, HALF, "down"),
    "u1": (0, HALF, "up"),
    "d0": (0, 0, "down"),
    "f0": (-1, 0, "up"),
    "f1": (1, HALF, "down"),
}
HOP_AT = {name: at for at, name in enumerate(HOPS)}


def kernel(
    go_hbm, w_hbm, x_hbm, dt_hbm, ld_hbm, b_hbm, c_hbm, skip_hbm,
    gi_ref, gs_ref, gd_ref, gb_ref, gc_ref,
    x_ref, dt_ref, ld_ref, b_ref, c_ref, skip_ref, in_s,
    wbuf, gbuf, accp, acco, pbufp, pbufo, xout, xin, gy, ge, ge_low, xs, xs_low, wts, dxs, cb, vsum, urow, dcol, qcol, dtile, dother,
    sfw, hin, hpair, rfw, ofw, hback, hsend, hbuf,
    sbw, qin, qpair, rbw, obw, qback, qsend, qbuf, dcp, dbp, prc, prb, gcs, gbs,
    w_s, w_r, g_s, g_r, z_s, z_r, p_s, p_r, o_s, o_r, x_s, x_r, e_s, e_r, f_s, f_r, h_s, h_r, l_s, l_r, q_s, q_r,
    rc_s, rc_r, ac_s, ac_r, rb_s, rb_r, ab_s, ab_r,
):
    seq = lax.axis_index("seq")
    head = lax.axis_index("head")
    xh = lax.div(seq, 8)
    yy = lax.rem(lax.div(seq, 2), 4)
    core = lax.rem(seq, 2)
    xl = lax.div(head, 8)
    zz = lax.rem(head, 8)
    other = seq + 1 - 2 * core
    beside = (1 - xl) * 8 + zz
    home = lax.rem(zz, 2)
    odd = lax.rem(zz + core, 2)

    own_w = pltpu.make_async_copy(w_hbm, wbuf.at[yy], in_s.at[6])
    own_w.start()
    loads = [
        pltpu.make_async_copy(src, dst, in_s.at[i])
        for i, (src, dst) in enumerate(
            (
                (ld_hbm, ld_ref),
                (dt_hbm, dt_ref),
                (x_hbm, x_ref),
                (b_hbm, b_ref),
                (c_hbm, c_ref),
                (skip_hbm, skip_ref),
            )
        )
    ]
    for load in loads:
        load.start()

    barrier = pltpu.get_barrier_semaphore()

    def greet(s, h):
        pl.semaphore_signal(
            barrier, inc=1, device_id={"seq": s, "head": h}, device_id_type=pl.DeviceIdType.MESH
        )

    over = seq + 8 - 16 * xh
    over_other = other + 8 - 16 * xh
    for h in (beside, head):
        greet(other, h)
        greet(over_other, h)
    greet(over, beside)
    for d in range(1, CHIPS):
        greet(lax.rem(seq + 2 * d, GROUP), head)
    for d in range(1, GROUP):
        greet(seq, lax.rem(head + d, GROUP))
    pl.semaphore_wait(barrier, 5 + CHIPS - 1 + GROUP - 1)

    sent = []

    def start(copy):
        copy.start()
        sent.append(copy)

    go_seq = xl * 8 + yy * 2 + home
    go_slot = gbuf.at[xh * 4 + lax.div(zz, 2), core]
    stays = jnp.logical_and(xl == xh, core == home)
    start(remote(go_hbm, go_slot, g_s.at[0], g_r.at[xh, core], go_seq, beside))
    inside = remote(go_hbm, go_slot, g_s.at[1], g_r.at[xh, core], go_seq, head)
    at_home = pltpu.make_async_copy(go_hbm, go_slot, g_s.at[2])

    @pl.when(jnp.logical_not(stays))
    def _():
        inside.start()

    @pl.when(stays)
    def _():
        at_home.start()

    def hop(name):
        dy, row, way = HOPS[name]
        at = HOP_AT[name]
        where = pl.ds(row, HALF)
        slot = wbuf.at[lax.rem(yy + dy + 4, 4), where]
        src = w_hbm.at[where] if dy == 0 else slot
        to = xh * 8 + lax.rem(yy + (1 if way == "up" else 3), 4) * 2 + core
        return remote(src, slot, w_s.at[at], w_r.at[at], to, head)

    def go(*names):
        for name in names:
            start(hop(name))

    def got(*names):
        for name in names:
            dy, row, way = HOPS[name]
            at = HOP_AT[name]
            dy = dy - 1 if way == "up" else dy + 1
            slot = wbuf.at[lax.rem(yy + dy + 4, 4), pl.ds(row, HALF)]
            remote(slot, slot, w_s.at[at], w_r.at[at], seq, head).wait_recv()

    go("u0", "d1", "u1", "d0")

    def group_at(group):
        return (1 - xh if group == 0 else xh) * 4

    def go_got(group):
        half_at = 1 - xh if group == 0 else xh
        for tok in (1 - core, core):
            slot = gbuf.at[group_at(group) + lax.div(zz, 2), tok]
            came = remote(slot, slot, g_s.at[0], g_r.at[half_at, tok], seq, head)
            if group == 1 and tok is core:

                @pl.when(stays)
                def _():
                    at_home.wait()

                @pl.when(jnp.logical_not(stays))
                def _():
                    came.wait_recv()

            else:
                came.wait_recv()

    def unit(group, way, d, half):
        z_from = lax.rem(zz + (8 - d if way == 0 else d), 8)
        k = group_at(group) + lax.div(z_from, 2)
        return gbuf.at[k, way] if half else gbuf.at[k]

    def z_hop(way, stage, group, is_odd):
        part = unit(group, way, 2 * stage + is_odd, is_odd and stage == 1)
        z_to = lax.rem(zz + (1 if way == 0 else 7), 8)
        return remote(
            part, part, z_s.at[way, stage, group], z_r.at[way, stage, group], seq, xl * 8 + z_to
        )

    def z_got(way, stage, group, is_odd):
        part = unit(group, way, 2 * stage + (1 if is_odd else 2), (not is_odd) and stage == 1)
        remote(
            part, part, z_s.at[way, stage, group], z_r.at[way, stage, group], seq, head
        ).wait_recv()

    def z_pass(stage_in, stage_out, group, is_odd):
        for way in range(2):
            z_got(way, stage_in, group, is_odd)
            if stage_out is not None:
                z_hop(way, stage_out, group, is_odd).start()

    rows_i = lax.broadcasted_iota(jnp.int32, (TOK, TOK), 0)
    cols_i = lax.broadcasted_iota(jnp.int32, (TOK, TOK), 1)
    causal = rows_i >= cols_i
    lower = jnp.where(causal, 1.0, 0.0).astype(F32)
    upper = jnp.where(rows_i <= cols_i, 1.0, 0.0).astype(F32)
    eye = jnp.where(rows_i == cols_i, 1.0, 0.0).astype(F32)
    lane = lax.broadcasted_iota(jnp.int32, (TOK, HEADS), 1)
    lane1 = lax.broadcasted_iota(jnp.int32, (HEADS, 1), 0)
    for load in loads:
        load.wait()
    dt_row = dt_ref[...]
    ld = ld_ref[...]
    run = exact(lower, ld, NT)
    run_row = exact(ld, upper, NN)
    dt = exact(eye, dt_row, NT)
    end = run[TOK - 1 : TOK, :]
    fade = jnp.exp(end - run)
    scale = dt * fade
    rise = jnp.exp(run)
    exp_end = jnp.exp(end)

    def z_begin(group):
        go_got(group)
        for way in range(2):
            z_hop(way, 0, group, 0).start()

    @pl.when(odd == 0)
    def _():
        z_begin(0)

    b_all = b_ref[...]
    c_all = c_ref[...]
    for h in range(HEADS):
        ch = slice(h * WIDTH, (h + 1) * WIDTH)
        scaled = x_ref[:, ch].astype(F32) * scale[:, h : h + 1]
        part, rest = split(scaled)
        xs[:, ch] = part
        xs_low[:, ch] = rest
        made = mm(part, b_all, TN) + mm(rest, b_all, TN)
        sfw[2 * h : 2 * h + 2] = made.reshape(2, SLICE, STATE)
        dtile[h] = jnp.broadcast_to(exp_end[:, h : h + 1], (8, 128))

    chip = lax.div(seq, 2)

    def tile(table, q):
        return table[core * (HEADS // 2) + q // 2, 0:1, 0:1]

    def pair_up(own, got_half, pair, first):
        for q in range(CHIPS):
            keep = jnp.where(first, tile(dother, q), 1.0)
            take = jnp.where(first, 1.0, tile(dtile, q))
            pair[q, 0:SLICE] = keep * own[core * CHIPS + q] + take * got_half[q]

    def pair_apart(back, own, got_half, send, out, first):
        for q in range(CHIPS):
            enters = back[q]
            mine = jnp.where(first, 1.0, tile(dother, q))
            here = jnp.where(first, 0.0, 1.0)
            out[core * CHIPS + q] = mine * enters + here * got_half[q]
            theirs = jnp.where(first, tile(dtile, q), 1.0)
            there = jnp.where(first, 1.0, 0.0)
            send[q] = theirs * enters + there * own[core * CHIPS + q]

    def half_of(buf, which):
        return buf.at[pl.ds(pl.multiple_of(which * CHIPS, CHIPS), CHIPS)]

    def to_chips(src, dst, ss, rs):
        for d in range(1, CHIPS):
            peer = lax.rem(chip + d, CHIPS)
            start(remote(src.at[peer], dst.at[chip], ss.at[d], rs.at[d], peer * 2 + core, head))
        dst[chip] = src[chip]

    def from_chips(dst, ss, rs):
        for d in range(1, CHIPS):
            peer = lax.rem(chip + CHIPS - d, CHIPS)
            remote(dst.at[peer], dst.at[peer], ss.at[d], rs.at[d], seq, head).wait_recv()

    first_fw = core == 0
    first_bw = core == 1
    tiles = remote(dtile, dother, e_s.at[0], e_r.at[0], other, head)
    start(tiles)
    halves = remote(half_of(sfw, 1 - core), hin, e_s.at[1], e_r.at[1], other, head)
    start(halves)

    cb[...] = mm(c_all, b_all, NT)
    got("u0")
    go("f0")
    got("d1")
    go("f1")

    @pl.when(odd == 1)
    def _():
        z_pass(0, 0, 0, 1)

    tiles.wait_recv()
    halves.wait_recv()
    pair_up(sfw, hin, hpair, first_fw)
    for q in range(CHIPS):
        both = tile(dtile, q) * tile(dother, q)
        hpair[q, SLICE : SLICE + 8] = jnp.broadcast_to(both, (8, STATE))

    @pl.when(odd == 0)
    def _():
        z_pass(0, 1, 0, 0)
        z_begin(1)

    @pl.when(odd == 1)
    def _():
        z_pass(1, 1, 0, 1)
        z_pass(0, 0, 1, 1)

    @pl.when(odd == 0)
    def _():
        z_pass(1, None, 0, 0)

    def scan(order, inbox, outbox):
        state = jnp.zeros((SLICE, STATE), F32)
        for q in order:
            outbox[q] = state
            state = state * rfw[q, SLICE : SLICE + 1, :] + inbox[q, 0:SLICE]

    def product(group, acc, n):
        total = None
        for k in range(4):
            left = gbuf[group_at(group) + k].reshape(2 * TOK, COLS)
            new = mm(left, wbuf[k, n * WIDE : (n + 1) * WIDE, :], NT)
            total = new if total is None else total + new
        acc[n] = total.reshape(2, TOK, WIDE)

    own_w.wait()
    got("u1", "d0", "f0", "f1")
    crossings = []

    def cross_over(n):
        swaps[n].wait_recv()
        xout[n] = (accp[n, core] + pbufp[n]).astype(BF16)
        cross = remote(xout.at[n], xin.at[n], x_s.at[n], x_r.at[n], over, head)
        start(cross)
        crossings.append(cross)

    swaps = []
    for n in range(CHUNKS):
        product(0, accp, n)
        swap = remote(accp.at[n, 1 - core], pbufp.at[n], p_s.at[n], p_r.at[n], other, head)
        start(swap)
        swaps.append(swap)
        if n > 0:
            cross_over(n - 1)
    cross_over(CHUNKS - 1)
    to_chips(hpair, rfw, f_s, f_r)

    @pl.when(odd == 1)
    def _():
        z_pass(1, 1, 1, 1)

    @pl.when(odd == 0)
    def _():
        z_pass(0, 1, 1, 0)
        z_pass(1, None, 1, 0)

    swaps = []
    for n in range(CHUNKS):
        product(1, acco, n)
        swap = remote(acco.at[n, 1 - core], pbufo.at[n], o_s.at[n], o_r.at[n], other, head)
        start(swap)
        swaps.append(swap)
    from_chips(rfw, f_s, f_r)
    scan(range(CHIPS), rfw, ofw)
    to_chips(ofw, hback, h_s, h_r)
    for n in range(CHUNKS):
        swaps[n].wait_recv()
        acco[n, core] = acco[n, core] + pbufo[n]

    for h in range(HEADS):
        ch = slice(h * WIDTH, (h + 1) * WIDTH)
        n, at = h // 2, slice((h % 2) * WIDTH, (h % 2 + 1) * WIDTH)
        if h % 2 == 0:
            crossings[n].wait_recv()
        up = (acco[n, core][:, at] + xin[n][:, at].astype(F32)).astype(BF16)
        gy[:, ch] = up
        part, rest = split(up.astype(F32) * rise[:, h : h + 1])
        ge[:, ch] = part
        ge_low[:, ch] = rest
        made = mm(part, c_all, TN) + mm(rest, c_all, TN)
        sbw[2 * h : 2 * h + 2] = made.reshape(2, SLICE, STATE)
    q_halves = remote(half_of(sbw, 1 - core), qin, e_s.at[3], e_r.at[3], other, head)
    start(q_halves)
    q_halves.wait_recv()
    pair_up(sbw, qin, qpair, first_bw)
    to_chips(qpair, rbw, l_s, l_r)
    from_chips(hback, h_s, h_r)
    pair_apart(hback, sfw, hin, hsend, hbuf, first_fw)
    h_swap = remote(hsend, half_of(hbuf, core), e_s.at[2], e_r.at[2], other, head)
    start(h_swap)

    vsum[...] = jnp.zeros((TOK, TOK), F32)
    dcol[...] = jnp.zeros((TOK, HEADS), F32)

    def inner(h):
        ch = slice(h * WIDTH, (h + 1) * WIDTH)
        weights = wts.at[h % 2]
        u_sum = [jnp.zeros((1, WIDTH), F32), jnp.zeros((1, TOK - WIDTH), F32)]
        for r in range(4):
            rows = slice(r * 64, (r + 1) * 64)
            wide = WIDTH if r < 2 else TOK
            gx = mm(gy[rows, ch], x_ref[:wide, ch], NT)
            gaps = run[rows, h : h + 1] - run_row[h : h + 1, :wide]
            decay = jnp.exp(jnp.where(causal[rows, :wide], gaps, -1e30))
            steps = dt_row[h : h + 1, :wide]
            mixed = decay * cb[rows, :wide]
            both = mixed * gx
            vsum[rows, :wide] += decay * gx * steps
            weights[rows, :wide] = (mixed * steps).astype(BF16)
            down = jnp.sum(both, axis=0, keepdims=True)
            u_sum[0] += down[:, :WIDTH]
            if r >= 2:
                u_sum[1] += down[:, WIDTH:]
            along = jnp.sum(both * steps, axis=1, keepdims=True)
            dcol[rows, :] += jnp.where(lane[rows] == h, along, 0.0)
        urow[h : h + 1, :WIDTH] = u_sum[0]
        urow[h : h + 1, WIDTH:] = u_sum[1]
        dxs[:WIDTH, ch] = mm(weights[:, :WIDTH], gy[:, ch], TN)
        dxs[WIDTH:, ch] = mm(weights[WIDTH:, WIDTH:], gy[WIDTH:, ch], TN)

    def inner_read(h):
        ch = slice(h * WIDTH, (h + 1) * WIDTH)
        part, rest = split(hbuf[2 * h : 2 * h + 2].reshape(WIDTH, STATE))
        read = mm(c_all, part, NT) + mm(c_all, rest, NT)
        along = rise[:, h : h + 1] * jnp.sum(gy[:, ch].astype(F32) * read, axis=1, keepdims=True)
        dcol[...] += jnp.where(lane == h, along, 0.0)

    for h in range(HEADS):
        inner(h)
    half = half_of(hbuf, 1 - core)
    remote(half, half, e_s.at[2], e_r.at[2], other, head).wait_recv()

    from_chips(rbw, l_s, l_r)
    scan(range(CHIPS - 1, -1, -1), rbw, obw)
    to_chips(obw, qback, q_s, q_r)

    for h in range(HEADS):
        inner_read(h)
    v_hi = vsum[...].astype(BF16)
    v_lo = (vsum[...] - v_hi.astype(F32)).astype(BF16)

    def spread(src, dst, ss, rs):
        for d in range(1, GROUP):
            peer = lax.rem(head + d, GROUP)
            part = src.at[pl.ds(pl.multiple_of(peer * PART, PART), PART)]
            start(remote(part, dst.at[head], ss.at[d], rs.at[d], seq, peer))
        dst[head] = src[pl.ds(pl.multiple_of(head * PART, PART), PART)]

    def collect(inbox, whole, ss, rs, ss2, rs2):
        for d in range(1, GROUP):
            peer = lax.rem(head + GROUP - d, GROUP)
            remote(inbox.at[peer], inbox.at[peer], ss.at[d], rs.at[d], seq, head).wait_recv()
        total = inbox[0].astype(F32)
        for i in range(1, GROUP):
            total = total + inbox[i].astype(F32)
        own = pl.ds(pl.multiple_of(head * PART, PART), PART)
        whole[own] = total.astype(whole.dtype)
        for d in range(1, GROUP):
            peer = lax.rem(head + d, GROUP)
            start(remote(whole.at[own], whole.at[own], ss2.at[d], rs2.at[d], seq, peer))

    def finish(whole, out, ss, rs):
        for d in range(1, GROUP):
            peer = lax.rem(head + GROUP - d, GROUP)
            part = whole.at[pl.ds(pl.multiple_of(peer * PART, PART), PART)]
            remote(part, part, ss.at[d], rs.at[d], seq, head).wait_recv()
        out[...] = whole[...].astype(F32)

    part, rest = split(hbuf[...].reshape(ROWS, STATE))
    dc = mm(v_hi, b_all, NN) + mm(v_lo, b_all, NN)
    dc += mm(ge[...], part, NN) + mm(ge_low[...], part, NN) + mm(ge[...], rest, NN)
    dcp[...] = dc.astype(BF16)
    spread(dcp, prc, rc_s, rc_r)

    from_chips(qback, q_s, q_r)
    pair_apart(qback, sbw, qin, qsend, qbuf, first_bw)
    q_swap = remote(qsend, half_of(qbuf, core), e_s.at[4], e_r.at[4], other, head)
    start(q_swap)
    half = half_of(qbuf, 1 - core)
    remote(half, half, e_s.at[4], e_r.at[4], other, head).wait_recv()
    part, rest = split(qbuf[...].reshape(ROWS, STATE))
    db = mm(v_hi, c_all, TN) + mm(v_lo, c_all, TN)
    db += mm(xs[...], part, NN) + mm(xs_low[...], part, NN) + mm(xs[...], rest, NN)
    dbp[...] = db.astype(BF16)
    spread(dbp, prb, rb_s, rb_r)
    collect(prc, gcs, rc_s, rc_r, ac_s, ac_r)

    qcol[...] = jnp.zeros((TOK, HEADS), F32)
    inner_hq = jnp.zeros((HEADS, 1), F32)
    for h in range(HEADS // 2):
        inner_hq = closing(h, lane, lane1, b_all, x_ref, gy, dxs, hbuf, qbuf, qcol, scale, skip_ref, gi_ref, inner_hq)
    collect(prb, gbs, rb_s, rb_r, ab_s, ab_r)
    for h in range(HEADS // 2, HEADS):
        inner_hq = closing(h, lane, lane1, b_all, x_ref, gy, dxs, hbuf, qbuf, qcol, scale, skip_ref, gi_ref, inner_hq)

    step_grad = urow[...] + exact(fade * qcol[...], eye, TN)
    gs_ref[...] = step_grad
    at_end = jnp.sum(exact(scale * qcol[...], eye, TN), axis=1, keepdims=True)
    at_end += jnp.exp(run_row[:, TOK - 1 : TOK]) * inner_hq
    gd_ref[...] = exact(exact(dcol[...], eye, TN) - dt_row * step_grad, lower, NN) + at_end

    finish(gcs, gc_ref, ac_s, ac_r)
    finish(gbs, gb_ref, ab_s, ab_r)

    for copy in sent:
        copy.wait_send()

    @pl.when(jnp.logical_not(stays))
    def _():
        inside.wait_send()

    for is_odd in range(2):

        @pl.when(odd == is_odd)
        def _():
            for stage in range(2):
                for way in range(2):
                    for group in range(2):
                        z_hop(way, stage, group, is_odd).wait_send()


def closing(h, lane, lane1, b_all, x_ref, gy, dxs, hbuf, qbuf, qcol, scale, skip_ref, gi_ref, inner_hq):
    ch = slice(h * WIDTH, (h + 1) * WIDTH)
    grad = qbuf[2 * h : 2 * h + 2].reshape(WIDTH, STATE)
    part, rest = split(grad)
    fed = mm(b_all, part, NT) + mm(b_all, rest, NT)
    met = jnp.sum(x_ref[:, ch].astype(F32) * fed, axis=1, keepdims=True)
    qcol[...] += jnp.where(lane == h, met, 0.0)
    gi_ref[:, ch] = (
        dxs[:, ch]
        + skip_ref[:, h : h + 1] * gy[:, ch].astype(F32)
        + scale[:, h : h + 1] * fed
    ).astype(BF16)
    state = hbuf[2 * h : 2 * h + 2].reshape(WIDTH, STATE)
    prod = state * grad
    total = jnp.sum(jnp.sum(prod, axis=0, keepdims=True), axis=1, keepdims=True)
    return inner_hq + jnp.where(lane1 == h, total, 0.0)


def hand_over(*refs):
    given, out, room, sems = refs[:5], refs[5:10], refs[10:15], refs[15]
    come = [pltpu.make_async_copy(given[i], room[i], sems.at[i]) for i in range(5)]
    leave = [pltpu.make_async_copy(room[i], out[i], sems.at[5 + i]) for i in range(5)]
    for copy in come:
        copy.start()
    for i in range(5):
        come[i].wait()
        leave[i].start()
    for copy in leave:
        copy.wait()


def local(grad_out, out_weight, ssm_input, step_size, log_decay, b_in, c_in, skip):
    vmem = pl.BlockSpec(memory_space=pltpu.VMEM)
    here = pl.BlockSpec(memory_space=pl.ANY)
    dma = pltpu.SemaphoreType.DMA
    slices = pltpu.VMEM((GROUP, SLICE, STATE), F32)
    halves = pltpu.VMEM((CHIPS, SLICE, STATE), F32)
    tagged = pltpu.VMEM((CHIPS, SLICE + 8, STATE), F32)
    short_parts = pltpu.VMEM((GROUP, PART, STATE), BF16)
    short_square = pltpu.VMEM((TOK, STATE), BF16)
    by_row = pltpu.VMEM((HEADS, TOK), F32)
    sums = pltpu.VMEM((CHUNKS, TOK, WIDE), F32)
    short = pltpu.VMEM((CHUNKS, TOK, WIDE), BF16)
    by_head = pltpu.VMEM((TOK, HEADS), F32)
    wide = pltpu.VMEM((TOK, ROWS), BF16)
    peers = dma((GROUP,))
    gi, gs, gd, gb, gc = pl.pallas_call(
        kernel,
        out_shape=(
            jax.ShapeDtypeStruct((TOK, ROWS), BF16),
            jax.ShapeDtypeStruct((HEADS, TOK), F32),
            jax.ShapeDtypeStruct((HEADS, TOK), F32),
            jax.ShapeDtypeStruct((TOK, STATE), F32),
            jax.ShapeDtypeStruct((TOK, STATE), F32),
        ),
        in_specs=[here] * 8,
        out_specs=[vmem] * 5,
        scratch_shapes=[
            wide,
            by_row, by_row,
            pltpu.VMEM((TOK, STATE), BF16), pltpu.VMEM((TOK, STATE), BF16),
            pltpu.VMEM((1, HEADS), F32),
            dma((7,)),
            pltpu.VMEM((4, ROWS, COLS), BF16),
            pltpu.VMEM((8, 2, TOK, COLS), BF16),
            pltpu.VMEM((CHUNKS, 2, TOK, WIDE), F32), pltpu.VMEM((CHUNKS, 2, TOK, WIDE), F32),
            sums, sums, short, short,
            wide,
            wide, wide,
            wide, wide,
            pltpu.VMEM((2, TOK, TOK), BF16),
            pltpu.VMEM((TOK, ROWS), F32),
            pltpu.VMEM((TOK, TOK), F32),
            pltpu.VMEM((TOK, TOK), F32),
            pltpu.VMEM((HEADS, TOK), F32),
            by_head,
            by_head,
            pltpu.VMEM((HEADS, 8, 128), F32),
            pltpu.VMEM((HEADS, 8, 128), F32),
            slices, halves, tagged, tagged, halves, halves, halves, slices,
            slices, halves, halves, halves, halves, halves, halves, slices,
            short_square, short_square,
            short_parts, short_parts,
            short_square, short_square,
            dma((len(HOPS),)), dma((len(HOPS),)),
            dma((3,)), dma((2, 2)),
            dma((2, 2, 2)), dma((2, 2, 2)),
            dma((CHUNKS,)), dma((CHUNKS,)),
            dma((CHUNKS,)), dma((CHUNKS,)),
            dma((CHUNKS,)), dma((CHUNKS,)),
        ] + [peers] * 18,
        compiler_params=pltpu.CompilerParams(
            collective_id=0, has_side_effects=True, vmem_limit_bytes=60 * 2**20
        ),
        name="layer_backward",
    )(
        grad_out, out_weight, ssm_input, step_size.T, log_decay.T, b_in, c_in, skip.reshape(1, HEADS)
    )
    gi, gs, gd, gb, gc = pl.pallas_call(
        hand_over,
        out_shape=tuple(jax.ShapeDtypeStruct(a.shape, a.dtype) for a in (gi, gs, gd, gb, gc)),
        in_specs=[here] * 5,
        out_specs=[here] * 5,
        scratch_shapes=[pltpu.VMEM(a.shape, a.dtype) for a in (gi, gs, gd, gb, gc)] + [dma((10,))],
        name="hand_over",
    )(gi, gs, gd, gb, gc)
    return gi, gs.T, gd.T, gb, gc


def solution(mesh):
    in_specs = (
        P("seq", "head"),
        P("head", "seq"),
        P("seq", "head"),
        P("seq", "head"),
        P("seq", "head"),
        P("seq", None),
        P("seq", None),
        P("head"),
    )
    out_specs = (
        P("seq", "head"),
        P("seq", "head"),
        P("seq", "head"),
        P("seq", None),
        P("seq", None),
    )
    return jax.shard_map(local, mesh=mesh, in_specs=in_specs, out_specs=out_specs, check_vma=False)
```

```python
import jax
import jax.numpy as jnp
from jax import lax
from jax.experimental import pallas as pl
from jax.experimental.pallas import tpu as pltpu
from jax.sharding import PartitionSpec as P

F32, BF16 = jnp.float32, jnp.bfloat16
HIGH = lax.Precision.HIGHEST
NN = (((1,), (0,)), ((), ()))
NT = (((1,), (1,)), ((), ()))
TN = (((0,), (0,)), ((), ()))

TOK = 256
HEADS = 8
WIDTH = 128
STATE = 256
ROWS = HEADS * WIDTH
COLS = 512
GROUP = 16
CHIPS = 8
SLICE = ROWS // GROUP
PART = TOK // GROUP
HALF = ROWS // 2
CHUNKS = 4
WIDE = ROWS // CHUNKS


def mm(a, b, dims):
    return lax.dot_general(a, b, dims, preferred_element_type=F32)


def exact(a, b, dims):
    return lax.dot_general(a, b, dims, precision=HIGH, preferred_element_type=F32)


def split(a):
    high = a.astype(BF16)
    return high, (a - high.astype(F32)).astype(BF16)


def remote(src, dst, send_sem, recv_sem, seq, head):
    return pltpu.make_async_remote_copy(
        src_ref=src,
        dst_ref=dst,
        send_sem=send_sem,
        recv_sem=recv_sem,
        device_id={"seq": seq, "head": head},
        device_id_type=pl.DeviceIdType.MESH,
    )


HOPS = {
    "u0": (0, 0, "up"),
    "d1": (0, HALF, "down"),
    "u1": (0, HALF, "up"),
    "d0": (0, 0, "down"),
    "f0": (-1, 0, "up"),
    "f1": (1, HALF, "down"),
}
HOP_AT = {name: at for at, name in enumerate(HOPS)}


def kernel(
    go_hbm, w_hbm, x_hbm, dt_hbm, ld_hbm, b_hbm, c_hbm, skip_hbm,
    gi_ref, gs_ref, gd_ref, gb_ref, gc_ref,
    x_ref, dt_ref, ld_ref, b_ref, c_ref, skip_ref, in_s,
    wbuf, gbuf, accp, acco, pbufp, pbufo, xout, xin, gy, ge, ge_low, xs, xs_low, wts, dxs, cb, vsum, urow, dcol, qcol, dtile, dother,
    sfw, hin, hpair, rfw, ofw, hback, hsend, hbuf,
    sbw, qin, qpair, rbw, obw, qback, qsend, qbuf, dcp, dbp, prc, prb, gcs, gbs,
    w_s, w_r, g_s, g_r, z_s, z_r, p_s, p_r, o_s, o_r, x_s, x_r, e_s, e_r, f_s, f_r, h_s, h_r, l_s, l_r, q_s, q_r,
    rc_s, rc_r, ac_s, ac_r, rb_s, rb_r, ab_s, ab_r,
):
    seq = lax.axis_index("seq")
    head = lax.axis_index("head")
    xh = lax.div(seq, 8)
    yy = lax.rem(lax.div(seq, 2), 4)
    core = lax.rem(seq, 2)
    xl = lax.div(head, 8)
    zz = lax.rem(head, 8)
    other = seq + 1 - 2 * core
    beside = (1 - xl) * 8 + zz
    home = lax.rem(zz, 2)
    odd = lax.rem(zz + core, 2)

    own_w = pltpu.make_async_copy(w_hbm, wbuf.at[yy], in_s.at[6])
    own_w.start()
    loads = [
        pltpu.make_async_copy(src, dst, in_s.at[i])
        for i, (src, dst) in enumerate(
            (
                (ld_hbm, ld_ref),
                (dt_hbm, dt_ref),
                (x_hbm, x_ref),
                (b_hbm, b_ref),
                (c_hbm, c_ref),
                (skip_hbm, skip_ref),
            )
        )
    ]
    for load in loads:
        load.start()

    barrier = pltpu.get_barrier_semaphore()

    def greet(s, h):
        pl.semaphore_signal(
            barrier, inc=1, device_id={"seq": s, "head": h}, device_id_type=pl.DeviceIdType.MESH
        )

    over = seq + 8 - 16 * xh
    over_other = other + 8 - 16 * xh
    for h in (beside, head):
        greet(other, h)
        greet(over_other, h)
    greet(over, beside)
    for d in range(1, CHIPS):
        greet(lax.rem(seq + 2 * d, GROUP), head)
    for d in range(1, GROUP):
        greet(seq, lax.rem(head + d, GROUP))
    pl.semaphore_wait(barrier, 5 + CHIPS - 1 + GROUP - 1)

    sent = []

    def start(copy):
        copy.start()
        sent.append(copy)

    go_seq = xl * 8 + yy * 2 + home
    go_slot = gbuf.at[xh * 4 + lax.div(zz, 2), core]
    stays = jnp.logical_and(xl == xh, core == home)
    start(remote(go_hbm, go_slot, g_s.at[0], g_r.at[xh, core], go_seq, beside))
    inside = remote(go_hbm, go_slot, g_s.at[1], g_r.at[xh, core], go_seq, head)
    at_home = pltpu.make_async_copy(go_hbm, go_slot, g_s.at[2])

    @pl.when(jnp.logical_not(stays))
    def _():
        inside.start()

    @pl.when(stays)
    def _():
        at_home.start()

    def hop(name):
        dy, row, way = HOPS[name]
        at = HOP_AT[name]
        where = pl.ds(row, HALF)
        slot = wbuf.at[lax.rem(yy + dy + 4, 4), where]
        src = w_hbm.at[where] if dy == 0 else slot
        to = xh * 8 + lax.rem(yy + (1 if way == "up" else 3), 4) * 2 + core
        return remote(src, slot, w_s.at[at], w_r.at[at], to, head)

    def go(*names):
        for name in names:
            start(hop(name))

    def got(*names):
        for name in names:
            dy, row, way = HOPS[name]
            at = HOP_AT[name]
            dy = dy - 1 if way == "up" else dy + 1
            slot = wbuf.at[lax.rem(yy + dy + 4, 4), pl.ds(row, HALF)]
            remote(slot, slot, w_s.at[at], w_r.at[at], seq, head).wait_recv()

    go("u0", "d1", "u1", "d0")

    def group_at(group):
        return (1 - xh if group == 0 else xh) * 4

    def go_got(group):
        half_at = 1 - xh if group == 0 else xh
        for tok in (1 - core, core):
            slot = gbuf.at[group_at(group) + lax.div(zz, 2), tok]
            came = remote(slot, slot, g_s.at[0], g_r.at[half_at, tok], seq, head)
            if group == 1 and tok is core:

                @pl.when(stays)
                def _():
                    at_home.wait()

                @pl.when(jnp.logical_not(stays))
                def _():
                    came.wait_recv()

            else:
                came.wait_recv()

    def unit(group, way, d, half):
        z_from = lax.rem(zz + (8 - d if way == 0 else d), 8)
        k = group_at(group) + lax.div(z_from, 2)
        return gbuf.at[k, way] if half else gbuf.at[k]

    def z_hop(way, stage, group, is_odd):
        part = unit(group, way, 2 * stage + is_odd, is_odd and stage == 1)
        z_to = lax.rem(zz + (1 if way == 0 else 7), 8)
        return remote(
            part, part, z_s.at[way, stage, group], z_r.at[way, stage, group], seq, xl * 8 + z_to
        )

    def z_got(way, stage, group, is_odd):
        part = unit(group, way, 2 * stage + (1 if is_odd else 2), (not is_odd) and stage == 1)
        remote(
            part, part, z_s.at[way, stage, group], z_r.at[way, stage, group], seq, head
        ).wait_recv()

    def z_pass(stage_in, stage_out, group, is_odd):
        for way in range(2):
            z_got(way, stage_in, group, is_odd)
            if stage_out is not None:
                z_hop(way, stage_out, group, is_odd).start()

    rows_i = lax.broadcasted_iota(jnp.int32, (TOK, TOK), 0)
    cols_i = lax.broadcasted_iota(jnp.int32, (TOK, TOK), 1)
    causal = rows_i >= cols_i
    lower = jnp.where(causal, 1.0, 0.0).astype(F32)
    upper = jnp.where(rows_i <= cols_i, 1.0, 0.0).astype(F32)
    eye = jnp.where(rows_i == cols_i, 1.0, 0.0).astype(F32)
    lane = lax.broadcasted_iota(jnp.int32, (TOK, HEADS), 1)
    lane1 = lax.broadcasted_iota(jnp.int32, (HEADS, 1), 0)
    for load in loads:
        load.wait()
    dt_row = dt_ref[...]
    ld = ld_ref[...]
    run = exact(lower, ld, NT)
    run_row = exact(ld, upper, NN)
    dt = exact(eye, dt_row, NT)
    end = run[TOK - 1 : TOK, :]
    fade = jnp.exp(end - run)
    scale = dt * fade
    rise = jnp.exp(run)
    exp_end = jnp.exp(end)

    def z_begin(group):
        go_got(group)
        for way in range(2):
            z_hop(way, 0, group, 0).start()

    @pl.when(odd == 0)
    def _():
        z_begin(0)

    b_all = b_ref[...]
    c_all = c_ref[...]
    for h in range(HEADS):
        ch = slice(h * WIDTH, (h + 1) * WIDTH)
        scaled = x_ref[:, ch].astype(F32) * scale[:, h : h + 1]
        part, rest = split(scaled)
        xs[:, ch] = part
        xs_low[:, ch] = rest
        made = mm(part, b_all, TN) + mm(rest, b_all, TN)
        sfw[2 * h : 2 * h + 2] = made.reshape(2, SLICE, STATE)
        dtile[h] = jnp.broadcast_to(exp_end[:, h : h + 1], (8, 128))

    chip = lax.div(seq, 2)

    def tile(table, q):
        return table[core * (HEADS // 2) + q // 2, 0:1, 0:1]

    def pair_up(own, got_half, pair, first):
        for q in range(CHIPS):
            keep = jnp.where(first, tile(dother, q), 1.0)
            take = jnp.where(first, 1.0, tile(dtile, q))
            pair[q, 0:SLICE] = keep * own[core * CHIPS + q] + take * got_half[q]

    def pair_apart(back, own, got_half, send, out, first):
        for q in range(CHIPS):
            enters = back[q]
            mine = jnp.where(first, 1.0, tile(dother, q))
            here = jnp.where(first, 0.0, 1.0)
            out[core * CHIPS + q] = mine * enters + here * got_half[q]
            theirs = jnp.where(first, tile(dtile, q), 1.0)
            there = jnp.where(first, 1.0, 0.0)
            send[q] = theirs * enters + there * own[core * CHIPS + q]

    def half_of(buf, which):
        return buf.at[pl.ds(pl.multiple_of(which * CHIPS, CHIPS), CHIPS)]

    def to_chips(src, dst, ss, rs):
        for d in range(1, CHIPS):
            peer = lax.rem(chip + d, CHIPS)
            start(remote(src.at[peer], dst.at[chip], ss.at[d], rs.at[d], peer * 2 + core, head))
        dst[chip] = src[chip]

    def from_chips(dst, ss, rs):
        for d in range(1, CHIPS):
            peer = lax.rem(chip + CHIPS - d, CHIPS)
            remote(dst.at[peer], dst.at[peer], ss.at[d], rs.at[d], seq, head).wait_recv()

    first_fw = core == 0
    first_bw = core == 1
    tiles = remote(dtile, dother, e_s.at[0], e_r.at[0], other, head)
    start(tiles)
    halves = remote(half_of(sfw, 1 - core), hin, e_s.at[1], e_r.at[1], other, head)
    start(halves)

    cb[...] = mm(c_all, b_all, NT)
    got("u0")
    go("f0")
    got("d1")
    go("f1")

    @pl.when(odd == 1)
    def _():
        z_pass(0, 0, 0, 1)

    tiles.wait_recv()
    halves.wait_recv()
    pair_up(sfw, hin, hpair, first_fw)
    for q in range(CHIPS):
        both = tile(dtile, q) * tile(dother, q)
        hpair[q, SLICE : SLICE + 8] = jnp.broadcast_to(both, (8, STATE))
    to_chips(hpair, rfw, f_s, f_r)

    @pl.when(odd == 0)
    def _():
        z_pass(0, 1, 0, 0)
        z_begin(1)

    @pl.when(odd == 1)
    def _():
        z_pass(1, 1, 0, 1)
        z_pass(0, 0, 1, 1)

    @pl.when(odd == 0)
    def _():
        z_pass(1, None, 0, 0)

    def scan(order, inbox, outbox):
        state = jnp.zeros((SLICE, STATE), F32)
        for q in order:
            outbox[q] = state
            state = state * rfw[q, SLICE : SLICE + 1, :] + inbox[q, 0:SLICE]

    def product(group, acc, n):
        total = None
        for k in range(4):
            left = gbuf[group_at(group) + k].reshape(2 * TOK, COLS)
            new = mm(left, wbuf[k, n * WIDE : (n + 1) * WIDE, :], NT)
            total = new if total is None else total + new
        acc[n] = total.reshape(2, TOK, WIDE)

    from_chips(rfw, f_s, f_r)
    scan(range(CHIPS), rfw, ofw)
    own_w.wait()
    got("u1", "d0", "f0", "f1")
    to_chips(ofw, hback, h_s, h_r)
    crossings = []

    def cross_over(n):
        swaps[n].wait_recv()
        xout[n] = (accp[n, core] + pbufp[n]).astype(BF16)
        cross = remote(xout.at[n], xin.at[n], x_s.at[n], x_r.at[n], over, head)
        start(cross)
        crossings.append(cross)

    swaps = []
    for n in range(CHUNKS):
        product(0, accp, n)
        swap = remote(accp.at[n, 1 - core], pbufp.at[n], p_s.at[n], p_r.at[n], other, head)
        start(swap)
        swaps.append(swap)
        if n > 0:
            cross_over(n - 1)
    cross_over(CHUNKS - 1)

    @pl.when(odd == 1)
    def _():
        z_pass(1, 1, 1, 1)

    @pl.when(odd == 0)
    def _():
        z_pass(0, 1, 1, 0)
        z_pass(1, None, 1, 0)

    swaps = []
    for n in range(CHUNKS):
        product(1, acco, n)
        swap = remote(acco.at[n, 1 - core], pbufo.at[n], o_s.at[n], o_r.at[n], other, head)
        start(swap)
        swaps.append(swap)
    for n in range(CHUNKS):
        swaps[n].wait_recv()
        acco[n, core] = acco[n, core] + pbufo[n]

    for h in range(HEADS):
        ch = slice(h * WIDTH, (h + 1) * WIDTH)
        n, at = h // 2, slice((h % 2) * WIDTH, (h % 2 + 1) * WIDTH)
        if h % 2 == 0:
            crossings[n].wait_recv()
        up = (acco[n, core][:, at] + xin[n][:, at].astype(F32)).astype(BF16)
        gy[:, ch] = up
        part, rest = split(up.astype(F32) * rise[:, h : h + 1])
        ge[:, ch] = part
        ge_low[:, ch] = rest
        made = mm(part, c_all, TN) + mm(rest, c_all, TN)
        sbw[2 * h : 2 * h + 2] = made.reshape(2, SLICE, STATE)
    q_halves = remote(half_of(sbw, 1 - core), qin, e_s.at[3], e_r.at[3], other, head)
    start(q_halves)
    q_halves.wait_recv()
    pair_up(sbw, qin, qpair, first_bw)
    to_chips(qpair, rbw, l_s, l_r)
    from_chips(hback, h_s, h_r)
    pair_apart(hback, sfw, hin, hsend, hbuf, first_fw)
    h_swap = remote(hsend, half_of(hbuf, core), e_s.at[2], e_r.at[2], other, head)
    start(h_swap)

    vsum[...] = jnp.zeros((TOK, TOK), F32)
    dcol[...] = jnp.zeros((TOK, HEADS), F32)

    def inner(h):
        ch = slice(h * WIDTH, (h + 1) * WIDTH)
        weights = wts.at[h % 2]
        u_sum = [jnp.zeros((1, WIDTH), F32), jnp.zeros((1, TOK - WIDTH), F32)]
        for r in range(4):
            rows = slice(r * 64, (r + 1) * 64)
            wide = WIDTH if r < 2 else TOK
            gx = mm(gy[rows, ch], x_ref[:wide, ch], NT)
            gaps = run[rows, h : h + 1] - run_row[h : h + 1, :wide]
            decay = jnp.exp(jnp.where(causal[rows, :wide], gaps, -1e30))
            steps = dt_row[h : h + 1, :wide]
            mixed = decay * cb[rows, :wide]
            both = mixed * gx
            vsum[rows, :wide] += decay * gx * steps
            weights[rows, :wide] = (mixed * steps).astype(BF16)
            down = jnp.sum(both, axis=0, keepdims=True)
            u_sum[0] += down[:, :WIDTH]
            if r >= 2:
                u_sum[1] += down[:, WIDTH:]
            along = jnp.sum(both * steps, axis=1, keepdims=True)
            dcol[rows, :] += jnp.where(lane[rows] == h, along, 0.0)
        urow[h : h + 1, :WIDTH] = u_sum[0]
        urow[h : h + 1, WIDTH:] = u_sum[1]
        dxs[:WIDTH, ch] = mm(weights[:, :WIDTH], gy[:, ch], TN)
        dxs[WIDTH:, ch] = mm(weights[WIDTH:, WIDTH:], gy[WIDTH:, ch], TN)

    def inner_read(h):
        ch = slice(h * WIDTH, (h + 1) * WIDTH)
        part, rest = split(hbuf[2 * h : 2 * h + 2].reshape(WIDTH, STATE))
        read = mm(c_all, part, NT) + mm(c_all, rest, NT)
        along = rise[:, h : h + 1] * jnp.sum(gy[:, ch].astype(F32) * read, axis=1, keepdims=True)
        dcol[...] += jnp.where(lane == h, along, 0.0)

    for h in range(HEADS):
        inner(h)
    half = half_of(hbuf, 1 - core)
    remote(half, half, e_s.at[2], e_r.at[2], other, head).wait_recv()

    from_chips(rbw, l_s, l_r)
    scan(range(CHIPS - 1, -1, -1), rbw, obw)
    to_chips(obw, qback, q_s, q_r)

    for h in range(HEADS):
        inner_read(h)
    v_hi = vsum[...].astype(BF16)
    v_lo = (vsum[...] - v_hi.astype(F32)).astype(BF16)

    def spread(src, dst, ss, rs):
        for d in range(1, GROUP):
            peer = lax.rem(head + d, GROUP)
            part = src.at[pl.ds(pl.multiple_of(peer * PART, PART), PART)]
            start(remote(part, dst.at[head], ss.at[d], rs.at[d], seq, peer))
        dst[head] = src[pl.ds(pl.multiple_of(head * PART, PART), PART)]

    def collect(inbox, whole, ss, rs, ss2, rs2):
        for d in range(1, GROUP):
            peer = lax.rem(head + GROUP - d, GROUP)
            remote(inbox.at[peer], inbox.at[peer], ss.at[d], rs.at[d], seq, head).wait_recv()
        total = inbox[0].astype(F32)
        for i in range(1, GROUP):
            total = total + inbox[i].astype(F32)
        own = pl.ds(pl.multiple_of(head * PART, PART), PART)
        whole[own] = total.astype(whole.dtype)
        for d in range(1, GROUP):
            peer = lax.rem(head + d, GROUP)
            start(remote(whole.at[own], whole.at[own], ss2.at[d], rs2.at[d], seq, peer))

    def finish(whole, out, ss, rs):
        for d in range(1, GROUP):
            peer = lax.rem(head + GROUP - d, GROUP)
            part = whole.at[pl.ds(pl.multiple_of(peer * PART, PART), PART)]
            remote(part, part, ss.at[d], rs.at[d], seq, head).wait_recv()
        out[...] = whole[...].astype(F32)

    part, rest = split(hbuf[...].reshape(ROWS, STATE))
    dc = mm(v_hi, b_all, NN) + mm(v_lo, b_all, NN)
    dc += mm(ge[...], part, NN) + mm(ge_low[...], part, NN) + mm(ge[...], rest, NN)
    dcp[...] = dc.astype(BF16)
    spread(dcp, prc, rc_s, rc_r)

    from_chips(qback, q_s, q_r)
    pair_apart(qback, sbw, qin, qsend, qbuf, first_bw)
    q_swap = remote(qsend, half_of(qbuf, core), e_s.at[4], e_r.at[4], other, head)
    start(q_swap)
    half = half_of(qbuf, 1 - core)
    remote(half, half, e_s.at[4], e_r.at[4], other, head).wait_recv()
    part, rest = split(qbuf[...].reshape(ROWS, STATE))
    db = mm(v_hi, c_all, TN) + mm(v_lo, c_all, TN)
    db += mm(xs[...], part, NN) + mm(xs_low[...], part, NN) + mm(xs[...], rest, NN)
    dbp[...] = db.astype(BF16)
    spread(dbp, prb, rb_s, rb_r)
    collect(prc, gcs, rc_s, rc_r, ac_s, ac_r)

    qcol[...] = jnp.zeros((TOK, HEADS), F32)
    inner_hq = jnp.zeros((HEADS, 1), F32)
    for h in range(HEADS // 2):
        inner_hq = closing(h, lane, lane1, b_all, x_ref, gy, dxs, hbuf, qbuf, qcol, scale, skip_ref, gi_ref, inner_hq)
    collect(prb, gbs, rb_s, rb_r, ab_s, ab_r)
    for h in range(HEADS // 2, HEADS):
        inner_hq = closing(h, lane, lane1, b_all, x_ref, gy, dxs, hbuf, qbuf, qcol, scale, skip_ref, gi_ref, inner_hq)

    step_grad = urow[...] + exact(fade * qcol[...], eye, TN)
    gs_ref[...] = step_grad
    at_end = jnp.sum(exact(scale * qcol[...], eye, TN), axis=1, keepdims=True)
    at_end += jnp.exp(run_row[:, TOK - 1 : TOK]) * inner_hq
    gd_ref[...] = exact(exact(dcol[...], eye, TN) - dt_row * step_grad, lower, NN) + at_end

    finish(gcs, gc_ref, ac_s, ac_r)
    finish(gbs, gb_ref, ab_s, ab_r)

    for copy in sent:
        copy.wait_send()

    @pl.when(jnp.logical_not(stays))
    def _():
        inside.wait_send()

    for is_odd in range(2):

        @pl.when(odd == is_odd)
        def _():
            for stage in range(2):
                for way in range(2):
                    for group in range(2):
                        z_hop(way, stage, group, is_odd).wait_send()


def closing(h, lane, lane1, b_all, x_ref, gy, dxs, hbuf, qbuf, qcol, scale, skip_ref, gi_ref, inner_hq):
    ch = slice(h * WIDTH, (h + 1) * WIDTH)
    grad = qbuf[2 * h : 2 * h + 2].reshape(WIDTH, STATE)
    part, rest = split(grad)
    fed = mm(b_all, part, NT) + mm(b_all, rest, NT)
    met = jnp.sum(x_ref[:, ch].astype(F32) * fed, axis=1, keepdims=True)
    qcol[...] += jnp.where(lane == h, met, 0.0)
    gi_ref[:, ch] = (
        dxs[:, ch]
        + skip_ref[:, h : h + 1] * gy[:, ch].astype(F32)
        + scale[:, h : h + 1] * fed
    ).astype(BF16)
    state = hbuf[2 * h : 2 * h + 2].reshape(WIDTH, STATE)
    prod = state * grad
    total = jnp.sum(jnp.sum(prod, axis=0, keepdims=True), axis=1, keepdims=True)
    return inner_hq + jnp.where(lane1 == h, total, 0.0)


def hand_over(*refs):
    given, out, room, sems = refs[:5], refs[5:10], refs[10:15], refs[15]
    come = [pltpu.make_async_copy(given[i], room[i], sems.at[i]) for i in range(5)]
    leave = [pltpu.make_async_copy(room[i], out[i], sems.at[5 + i]) for i in range(5)]
    for copy in come:
        copy.start()
    for i in range(5):
        come[i].wait()
        leave[i].start()
    for copy in leave:
        copy.wait()


def local(grad_out, out_weight, ssm_input, step_size, log_decay, b_in, c_in, skip):
    vmem = pl.BlockSpec(memory_space=pltpu.VMEM)
    here = pl.BlockSpec(memory_space=pl.ANY)
    dma = pltpu.SemaphoreType.DMA
    slices = pltpu.VMEM((GROUP, SLICE, STATE), F32)
    halves = pltpu.VMEM((CHIPS, SLICE, STATE), F32)
    tagged = pltpu.VMEM((CHIPS, SLICE + 8, STATE), F32)
    short_parts = pltpu.VMEM((GROUP, PART, STATE), BF16)
    short_square = pltpu.VMEM((TOK, STATE), BF16)
    by_row = pltpu.VMEM((HEADS, TOK), F32)
    sums = pltpu.VMEM((CHUNKS, TOK, WIDE), F32)
    short = pltpu.VMEM((CHUNKS, TOK, WIDE), BF16)
    by_head = pltpu.VMEM((TOK, HEADS), F32)
    wide = pltpu.VMEM((TOK, ROWS), BF16)
    peers = dma((GROUP,))
    gi, gs, gd, gb, gc = pl.pallas_call(
        kernel,
        out_shape=(
            jax.ShapeDtypeStruct((TOK, ROWS), BF16),
            jax.ShapeDtypeStruct((HEADS, TOK), F32),
            jax.ShapeDtypeStruct((HEADS, TOK), F32),
            jax.ShapeDtypeStruct((TOK, STATE), F32),
            jax.ShapeDtypeStruct((TOK, STATE), F32),
        ),
        in_specs=[here] * 8,
        out_specs=[vmem] * 5,
        scratch_shapes=[
            wide,
            by_row, by_row,
            pltpu.VMEM((TOK, STATE), BF16), pltpu.VMEM((TOK, STATE), BF16),
            pltpu.VMEM((1, HEADS), F32),
            dma((7,)),
            pltpu.VMEM((4, ROWS, COLS), BF16),
            pltpu.VMEM((8, 2, TOK, COLS), BF16),
            pltpu.VMEM((CHUNKS, 2, TOK, WIDE), F32), pltpu.VMEM((CHUNKS, 2, TOK, WIDE), F32),
            sums, sums, short, short,
            wide,
            wide, wide,
            wide, wide,
            pltpu.VMEM((2, TOK, TOK), BF16),
            pltpu.VMEM((TOK, ROWS), F32),
            pltpu.VMEM((TOK, TOK), F32),
            pltpu.VMEM((TOK, TOK), F32),
            pltpu.VMEM((HEADS, TOK), F32),
            by_head,
            by_head,
            pltpu.VMEM((HEADS, 8, 128), F32),
            pltpu.VMEM((HEADS, 8, 128), F32),
            slices, halves, tagged, tagged, halves, halves, halves, slices,
            slices, halves, halves, halves, halves, halves, halves, slices,
            short_square, short_square,
            short_parts, short_parts,
            short_square, short_square,
            dma((len(HOPS),)), dma((len(HOPS),)),
            dma((3,)), dma((2, 2)),
            dma((2, 2, 2)), dma((2, 2, 2)),
            dma((CHUNKS,)), dma((CHUNKS,)),
            dma((CHUNKS,)), dma((CHUNKS,)),
            dma((CHUNKS,)), dma((CHUNKS,)),
        ] + [peers] * 18,
        compiler_params=pltpu.CompilerParams(
            collective_id=0, has_side_effects=True, vmem_limit_bytes=60 * 2**20
        ),
        name="layer_backward",
    )(
        grad_out, out_weight, ssm_input, step_size.T, log_decay.T, b_in, c_in, skip.reshape(1, HEADS)
    )
    gi, gs, gd, gb, gc = pl.pallas_call(
        hand_over,
        out_shape=tuple(jax.ShapeDtypeStruct(a.shape, a.dtype) for a in (gi, gs, gd, gb, gc)),
        in_specs=[here] * 5,
        out_specs=[here] * 5,
        scratch_shapes=[pltpu.VMEM(a.shape, a.dtype) for a in (gi, gs, gd, gb, gc)] + [dma((10,))],
        name="hand_over",
    )(gi, gs, gd, gb, gc)
    return gi, gs.T, gd.T, gb, gc


def solution(mesh):
    in_specs = (
        P("seq", "head"),
        P("head", "seq"),
        P("seq", "head"),
        P("seq", "head"),
        P("seq", "head"),
        P("seq", None),
        P("seq", None),
        P("head"),
    )
    out_specs = (
        P("seq", "head"),
        P("seq", "head"),
        P("seq", "head"),
        P("seq", None),
        P("seq", None),
    )
    return jax.shard_map(local, mesh=mesh, in_specs=in_specs, out_specs=out_specs, check_vma=False)
```

```python
import jax
import jax.numpy as jnp
from jax import lax
from jax.experimental import pallas as pl
from jax.experimental.pallas import tpu as pltpu
from jax.sharding import PartitionSpec as P

F32, BF16 = jnp.float32, jnp.bfloat16
HIGH = lax.Precision.HIGHEST
NN = (((1,), (0,)), ((), ()))
NT = (((1,), (1,)), ((), ()))
TN = (((0,), (0,)), ((), ()))

TOK = 256
HEADS = 8
WIDTH = 128
STATE = 256
ROWS = HEADS * WIDTH
COLS = 512
GROUP = 16
CHIPS = 8
SLICE = ROWS // GROUP
PART = TOK // GROUP
HALF = ROWS // 2
CHUNKS = 4
WIDE = ROWS // CHUNKS


def mm(a, b, dims):
    return lax.dot_general(a, b, dims, preferred_element_type=F32)


def exact(a, b, dims):
    return lax.dot_general(a, b, dims, precision=HIGH, preferred_element_type=F32)


def split(a):
    high = a.astype(BF16)
    return high, (a - high.astype(F32)).astype(BF16)


def remote(src, dst, send_sem, recv_sem, seq, head):
    return pltpu.make_async_remote_copy(
        src_ref=src,
        dst_ref=dst,
        send_sem=send_sem,
        recv_sem=recv_sem,
        device_id={"seq": seq, "head": head},
        device_id_type=pl.DeviceIdType.MESH,
    )


HOPS = {
    "u0": (0, 0, "up"),
    "d1": (0, HALF, "down"),
    "u1": (0, HALF, "up"),
    "d0": (0, 0, "down"),
    "f0": (-1, 0, "up"),
    "f1": (1, HALF, "down"),
}
HOP_AT = {name: at for at, name in enumerate(HOPS)}


def kernel(
    go_hbm, w_hbm, x_hbm, dt_hbm, ld_hbm, b_hbm, c_hbm, skip_hbm,
    gi_ref, gs_ref, gd_ref, gb_ref, gc_ref,
    x_ref, dt_ref, ld_ref, b_ref, c_ref, skip_ref, in_s,
    wbuf, gbuf, accp, acco, pbufp, pbufo, xout, xin, gy, ge, ge_low, xs, xs_low, wts, dxs, cb, vsum, urow, dcol, qcol, dtile, dother,
    sfw, hin, hpair, rfw, ofw, hback, hsend, hbuf,
    sbw, qin, qpair, rbw, obw, qback, qsend, qbuf, dcp, dbp, prc, prb, gcs, gbs,
    w_s, w_r, g_s, g_r, z_s, z_r, p_s, p_r, o_s, o_r, x_s, x_r, e_s, e_r, f_s, f_r, h_s, h_r, l_s, l_r, q_s, q_r,
    rc_s, rc_r, ac_s, ac_r, rb_s, rb_r, ab_s, ab_r,
):
    seq = lax.axis_index("seq")
    head = lax.axis_index("head")
    xh = lax.div(seq, 8)
    yy = lax.rem(lax.div(seq, 2), 4)
    core = lax.rem(seq, 2)
    xl = lax.div(head, 8)
    zz = lax.rem(head, 8)
    other = seq + 1 - 2 * core
    beside = (1 - xl) * 8 + zz
    home = lax.rem(zz, 2)
    odd = lax.rem(zz + core, 2)

    own_w = pltpu.make_async_copy(w_hbm, wbuf.at[yy], in_s.at[6])
    own_w.start()
    loads = [
        pltpu.make_async_copy(src, dst, in_s.at[i])
        for i, (src, dst) in enumerate(
            (
                (ld_hbm, ld_ref),
                (dt_hbm, dt_ref),
                (x_hbm, x_ref),
                (b_hbm, b_ref),
                (c_hbm, c_ref),
                (skip_hbm, skip_ref),
            )
        )
    ]
    for load in loads:
        load.start()

    barrier = pltpu.get_barrier_semaphore()

    def greet(s, h):
        pl.semaphore_signal(
            barrier, inc=1, device_id={"seq": s, "head": h}, device_id_type=pl.DeviceIdType.MESH
        )

    over = seq + 8 - 16 * xh
    over_other = other + 8 - 16 * xh
    for h in (beside, head):
        greet(other, h)
        greet(over_other, h)
    greet(over, beside)
    for d in range(1, CHIPS):
        greet(lax.rem(seq + 2 * d, GROUP), head)
    for d in range(1, GROUP):
        greet(seq, lax.rem(head + d, GROUP))
    pl.semaphore_wait(barrier, 5 + CHIPS - 1 + GROUP - 1)

    sent = []

    def start(copy):
        copy.start()
        sent.append(copy)

    go_seq = xl * 8 + yy * 2 + home
    go_slot = gbuf.at[xh * 4 + lax.div(zz, 2), core]
    stays = jnp.logical_and(xl == xh, core == home)
    start(remote(go_hbm, go_slot, g_s.at[0], g_r.at[xh, core], go_seq, beside))
    inside = remote(go_hbm, go_slot, g_s.at[1], g_r.at[xh, core], go_seq, head)
    at_home = pltpu.make_async_copy(go_hbm, go_slot, g_s.at[2])

    @pl.when(jnp.logical_not(stays))
    def _():
        inside.start()

    @pl.when(stays)
    def _():
        at_home.start()

    def hop(name):
        dy, row, way = HOPS[name]
        at = HOP_AT[name]
        where = pl.ds(row, HALF)
        slot = wbuf.at[lax.rem(yy + dy + 4, 4), where]
        src = w_hbm.at[where] if dy == 0 else slot
        to = xh * 8 + lax.rem(yy + (1 if way == "up" else 3), 4) * 2 + core
        return remote(src, slot, w_s.at[at], w_r.at[at], to, head)

    def go(*names):
        for name in names:
            start(hop(name))

    def got(*names):
        for name in names:
            dy, row, way = HOPS[name]
            at = HOP_AT[name]
            dy = dy - 1 if way == "up" else dy + 1
            slot = wbuf.at[lax.rem(yy + dy + 4, 4), pl.ds(row, HALF)]
            remote(slot, slot, w_s.at[at], w_r.at[at], seq, head).wait_recv()

    go("u0", "d1", "u1", "d0")

    def group_at(group):
        return (1 - xh if group == 0 else xh) * 4

    def go_got(group):
        half_at = 1 - xh if group == 0 else xh
        for tok in (1 - core, core):
            slot = gbuf.at[group_at(group) + lax.div(zz, 2), tok]
            came = remote(slot, slot, g_s.at[0], g_r.at[half_at, tok], seq, head)
            if group == 1 and tok is core:

                @pl.when(stays)
                def _():
                    at_home.wait()

                @pl.when(jnp.logical_not(stays))
                def _():
                    came.wait_recv()

            else:
                came.wait_recv()

    def unit(group, way, d, half):
        z_from = lax.rem(zz + (8 - d if way == 0 else d), 8)
        k = group_at(group) + lax.div(z_from, 2)
        return gbuf.at[k, way] if half else gbuf.at[k]

    def z_hop(way, stage, group, is_odd):
        part = unit(group, way, 2 * stage + is_odd, is_odd and stage == 1)
        z_to = lax.rem(zz + (1 if way == 0 else 7), 8)
        return remote(
            part, part, z_s.at[way, stage, group], z_r.at[way, stage, group], seq, xl * 8 + z_to
        )

    def z_got(way, stage, group, is_odd):
        part = unit(group, way, 2 * stage + (1 if is_odd else 2), (not is_odd) and stage == 1)
        remote(
            part, part, z_s.at[way, stage, group], z_r.at[way, stage, group], seq, head
        ).wait_recv()

    def z_pass(stage_in, stage_out, group, is_odd):
        for way in range(2):
            z_got(way, stage_in, group, is_odd)
            if stage_out is not None:
                z_hop(way, stage_out, group, is_odd).start()

    rows_i = lax.broadcasted_iota(jnp.int32, (TOK, TOK), 0)
    cols_i = lax.broadcasted_iota(jnp.int32, (TOK, TOK), 1)
    causal = rows_i >= cols_i
    lower = jnp.where(causal, 1.0, 0.0).astype(F32)
    upper = jnp.where(rows_i <= cols_i, 1.0, 0.0).astype(F32)
    eye = jnp.where(rows_i == cols_i, 1.0, 0.0).astype(F32)
    lane = lax.broadcasted_iota(jnp.int32, (TOK, HEADS), 1)
    lane1 = lax.broadcasted_iota(jnp.int32, (HEADS, 1), 0)
    for load in loads:
        load.wait()
    dt_row = dt_ref[...]
    ld = ld_ref[...]
    run = exact(lower, ld, NT)
    run_row = exact(ld, upper, NN)
    dt = exact(eye, dt_row, NT)
    end = run[TOK - 1 : TOK, :]
    fade = jnp.exp(end - run)
    scale = dt * fade
    rise = jnp.exp(run)
    exp_end = jnp.exp(end)

    def z_begin(group):
        go_got(group)
        for way in range(2):
            z_hop(way, 0, group, 0).start()

    @pl.when(odd == 0)
    def _():
        z_begin(0)

    b_all = b_ref[...]
    c_all = c_ref[...]
    for h in range(HEADS):
        ch = slice(h * WIDTH, (h + 1) * WIDTH)
        scaled = x_ref[:, ch].astype(F32) * scale[:, h : h + 1]
        part, rest = split(scaled)
        xs[:, ch] = part
        xs_low[:, ch] = rest
        made = mm(part, b_all, TN) + mm(rest, b_all, TN)
        sfw[2 * h : 2 * h + 2] = made.reshape(2, SLICE, STATE)
        dtile[h] = jnp.broadcast_to(exp_end[:, h : h + 1], (8, 128))

    chip = lax.div(seq, 2)

    def tile(table, q):
        return table[core * (HEADS // 2) + q // 2, 0:1, 0:1]

    def pair_up(own, got_half, pair, first):
        for q in range(CHIPS):
            keep = jnp.where(first, tile(dother, q), 1.0)
            take = jnp.where(first, 1.0, tile(dtile, q))
            pair[q, 0:SLICE] = keep * own[core * CHIPS + q] + take * got_half[q]

    def pair_apart(back, own, got_half, send, out, first):
        for q in range(CHIPS):
            enters = back[q]
            mine = jnp.where(first, 1.0, tile(dother, q))
            here = jnp.where(first, 0.0, 1.0)
            out[core * CHIPS + q] = mine * enters + here * got_half[q]
            theirs = jnp.where(first, tile(dtile, q), 1.0)
            there = jnp.where(first, 1.0, 0.0)
            send[q] = theirs * enters + there * own[core * CHIPS + q]

    def half_of(buf, which):
        return buf.at[pl.ds(pl.multiple_of(which * CHIPS, CHIPS), CHIPS)]

    def to_chips(src, dst, ss, rs):
        for d in range(1, CHIPS):
            peer = lax.rem(chip + d, CHIPS)
            start(remote(src.at[peer], dst.at[chip], ss.at[d], rs.at[d], peer * 2 + core, head))
        dst[chip] = src[chip]

    def from_chips(dst, ss, rs):
        for d in range(1, CHIPS):
            peer = lax.rem(chip + CHIPS - d, CHIPS)
            remote(dst.at[peer], dst.at[peer], ss.at[d], rs.at[d], seq, head).wait_recv()

    first_fw = core == 0
    first_bw = core == 1
    tiles = remote(dtile, dother, e_s.at[0], e_r.at[0], other, head)
    start(tiles)
    halves = remote(half_of(sfw, 1 - core), hin, e_s.at[1], e_r.at[1], other, head)
    start(halves)

    cb[...] = mm(c_all, b_all, NT)
    got("u0")
    go("f0")
    got("d1")
    go("f1")

    @pl.when(odd == 1)
    def _():
        z_pass(0, 0, 0, 1)

    tiles.wait_recv()
    halves.wait_recv()
    pair_up(sfw, hin, hpair, first_fw)
    for q in range(CHIPS):
        both = tile(dtile, q) * tile(dother, q)
        hpair[q, SLICE : SLICE + 8] = jnp.broadcast_to(both, (8, STATE))

    @pl.when(odd == 0)
    def _():
        z_pass(0, 1, 0, 0)
        z_begin(1)

    @pl.when(odd == 1)
    def _():
        z_pass(1, 1, 0, 1)
        z_pass(0, 0, 1, 1)

    @pl.when(odd == 0)
    def _():
        z_pass(1, None, 0, 0)

    def scan(order, inbox, outbox):
        state = jnp.zeros((SLICE, STATE), F32)
        for q in order:
            outbox[q] = state
            state = state * rfw[q, SLICE : SLICE + 1, :] + inbox[q, 0:SLICE]

    def product(group, acc, n):
        total = None
        for k in range(4):
            left = gbuf[group_at(group) + k].reshape(2 * TOK, COLS)
            new = mm(left, wbuf[k, n * WIDE : (n + 1) * WIDE, :], NT)
            total = new if total is None else total + new
        acc[n] = total.reshape(2, TOK, WIDE)

    own_w.wait()
    got("u1", "d0", "f0", "f1")
    crossings = []

    def cross_over(n):
        swaps[n].wait_recv()
        xout[n] = (accp[n, core] + pbufp[n]).astype(BF16)
        cross = remote(xout.at[n], xin.at[n], x_s.at[n], x_r.at[n], over, head)
        start(cross)
        crossings.append(cross)

    swaps = []
    for n in range(CHUNKS):
        product(0, accp, n)
        swap = remote(accp.at[n, 1 - core], pbufp.at[n], p_s.at[n], p_r.at[n], other, head)
        start(swap)
        swaps.append(swap)
        if n > 0:
            cross_over(n - 1)
    cross_over(CHUNKS - 1)
    to_chips(hpair, rfw, f_s, f_r)

    @pl.when(odd == 1)
    def _():
        z_pass(1, 1, 1, 1)

    @pl.when(odd == 0)
    def _():
        z_pass(0, 1, 1, 0)
        z_pass(1, None, 1, 0)

    swaps = []
    for n in range(CHUNKS):
        product(1, acco, n)
        swap = remote(acco.at[n, 1 - core], pbufo.at[n], o_s.at[n], o_r.at[n], other, head)
        start(swap)
        swaps.append(swap)
    from_chips(rfw, f_s, f_r)
    scan(range(CHIPS), rfw, ofw)
    to_chips(ofw, hback, h_s, h_r)
    for n in range(CHUNKS):
        swaps[n].wait_recv()
        acco[n, core] = acco[n, core] + pbufo[n]

    def q_part(i):
        part = pl.ds(pl.multiple_of((1 - core) * CHIPS + 4 * i, 4), 4)
        at = 3 + 2 * i
        return remote(sbw.at[part], qin.at[pl.ds(4 * i, 4)], e_s.at[at], e_r.at[at], other, head)

    for h in range(HEADS):
        ch = slice(h * WIDTH, (h + 1) * WIDTH)
        n, at = h // 2, slice((h % 2) * WIDTH, (h % 2 + 1) * WIDTH)
        if h % 2 == 0:
            crossings[n].wait_recv()
        up = (acco[n, core][:, at] + xin[n][:, at].astype(F32)).astype(BF16)
        gy[:, ch] = up
        part, rest = split(up.astype(F32) * rise[:, h : h + 1])
        ge[:, ch] = part
        ge_low[:, ch] = rest
        made = mm(part, c_all, TN) + mm(rest, c_all, TN)
        sbw[2 * h : 2 * h + 2] = made.reshape(2, SLICE, STATE)
        if h % 2 == 1:

            @pl.when(core == 1 - n // 2)
            def _():
                q_part(n % 2).start()

    for i in range(2):
        q_part(i).wait_recv()
    pair_up(sbw, qin, qpair, first_bw)
    to_chips(qpair, rbw, l_s, l_r)
    from_chips(hback, h_s, h_r)
    pair_apart(hback, sfw, hin, hsend, hbuf, first_fw)
    h_swap = remote(hsend, half_of(hbuf, core), e_s.at[2], e_r.at[2], other, head)
    start(h_swap)

    vsum[...] = jnp.zeros((TOK, TOK), F32)
    dcol[...] = jnp.zeros((TOK, HEADS), F32)

    def inner(h):
        ch = slice(h * WIDTH, (h + 1) * WIDTH)
        weights = wts.at[h % 2]
        u_sum = [jnp.zeros((1, WIDTH), F32), jnp.zeros((1, TOK - WIDTH), F32)]
        for r in range(4):
            rows = slice(r * 64, (r + 1) * 64)
            wide = WIDTH if r < 2 else TOK
            gx = mm(gy[rows, ch], x_ref[:wide, ch], NT)
            gaps = run[rows, h : h + 1] - run_row[h : h + 1, :wide]
            decay = jnp.exp(jnp.where(causal[rows, :wide], gaps, -1e30))
            steps = dt_row[h : h + 1, :wide]
            mixed = decay * cb[rows, :wide]
            both = mixed * gx
            vsum[rows, :wide] += decay * gx * steps
            weights[rows, :wide] = (mixed * steps).astype(BF16)
            down = jnp.sum(both, axis=0, keepdims=True)
            u_sum[0] += down[:, :WIDTH]
            if r >= 2:
                u_sum[1] += down[:, WIDTH:]
            along = jnp.sum(both * steps, axis=1, keepdims=True)
            dcol[rows, :] += jnp.where(lane[rows] == h, along, 0.0)
        urow[h : h + 1, :WIDTH] = u_sum[0]
        urow[h : h + 1, WIDTH:] = u_sum[1]
        dxs[:WIDTH, ch] = mm(weights[:, :WIDTH], gy[:, ch], TN)
        dxs[WIDTH:, ch] = mm(weights[WIDTH:, WIDTH:], gy[WIDTH:, ch], TN)

    def inner_read(h):
        ch = slice(h * WIDTH, (h + 1) * WIDTH)
        part, rest = split(hbuf[2 * h : 2 * h + 2].reshape(WIDTH, STATE))
        read = mm(c_all, part, NT) + mm(c_all, rest, NT)
        along = rise[:, h : h + 1] * jnp.sum(gy[:, ch].astype(F32) * read, axis=1, keepdims=True)
        dcol[...] += jnp.where(lane == h, along, 0.0)

    for h in range(HEADS):
        inner(h)
    half = half_of(hbuf, 1 - core)
    remote(half, half, e_s.at[2], e_r.at[2], other, head).wait_recv()

    from_chips(rbw, l_s, l_r)
    scan(range(CHIPS - 1, -1, -1), rbw, obw)
    to_chips(obw, qback, q_s, q_r)

    for h in range(HEADS):
        inner_read(h)
    v_hi = vsum[...].astype(BF16)
    v_lo = (vsum[...] - v_hi.astype(F32)).astype(BF16)

    def spread(src, dst, ss, rs):
        for d in range(1, GROUP):
            peer = lax.rem(head + d, GROUP)
            part = src.at[pl.ds(pl.multiple_of(peer * PART, PART), PART)]
            start(remote(part, dst.at[head], ss.at[d], rs.at[d], seq, peer))
        dst[head] = src[pl.ds(pl.multiple_of(head * PART, PART), PART)]

    def collect(inbox, whole, ss, rs, ss2, rs2):
        for d in range(1, GROUP):
            peer = lax.rem(head + GROUP - d, GROUP)
            remote(inbox.at[peer], inbox.at[peer], ss.at[d], rs.at[d], seq, head).wait_recv()
        total = inbox[0].astype(F32)
        for i in range(1, GROUP):
            total = total + inbox[i].astype(F32)
        own = pl.ds(pl.multiple_of(head * PART, PART), PART)
        whole[own] = total.astype(whole.dtype)
        for d in range(1, GROUP):
            peer = lax.rem(head + d, GROUP)
            start(remote(whole.at[own], whole.at[own], ss2.at[d], rs2.at[d], seq, peer))

    def finish(whole, out, ss, rs):
        for d in range(1, GROUP):
            peer = lax.rem(head + GROUP - d, GROUP)
            part = whole.at[pl.ds(pl.multiple_of(peer * PART, PART), PART)]
            remote(part, part, ss.at[d], rs.at[d], seq, head).wait_recv()
        out[...] = whole[...].astype(F32)

    part, rest = split(hbuf[...].reshape(ROWS, STATE))
    dc = mm(v_hi, b_all, NN) + mm(v_lo, b_all, NN)
    dc += mm(ge[...], part, NN) + mm(ge_low[...], part, NN) + mm(ge[...], rest, NN)
    dcp[...] = dc.astype(BF16)
    spread(dcp, prc, rc_s, rc_r)
    db = mm(v_hi, c_all, TN) + mm(v_lo, c_all, TN)

    from_chips(qback, q_s, q_r)
    pair_apart(qback, sbw, qin, qsend, qbuf, first_bw)
    q_swap = remote(qsend, half_of(qbuf, core), e_s.at[4], e_r.at[4], other, head)
    start(q_swap)

    def fed_by(which):
        cols = pl.ds(pl.multiple_of(which * HALF, HALF), HALF)
        part, rest = split(half_of(qbuf, which)[...].reshape(HALF, STATE))
        return mm(xs[:, cols], part, NN) + mm(xs_low[:, cols], part, NN) + mm(xs[:, cols], rest, NN)

    db += fed_by(core)
    half = half_of(qbuf, 1 - core)
    remote(half, half, e_s.at[4], e_r.at[4], other, head).wait_recv()
    db += fed_by(1 - core)
    dbp[...] = db.astype(BF16)
    spread(dbp, prb, rb_s, rb_r)
    collect(prc, gcs, rc_s, rc_r, ac_s, ac_r)

    qcol[...] = jnp.zeros((TOK, HEADS), F32)
    inner_hq = jnp.zeros((HEADS, 1), F32)
    for h in range(HEADS // 2):
        inner_hq = closing(h, lane, lane1, b_all, x_ref, gy, dxs, hbuf, qbuf, qcol, scale, skip_ref, gi_ref, inner_hq)
    collect(prb, gbs, rb_s, rb_r, ab_s, ab_r)
    for h in range(HEADS // 2, HEADS):
        inner_hq = closing(h, lane, lane1, b_all, x_ref, gy, dxs, hbuf, qbuf, qcol, scale, skip_ref, gi_ref, inner_hq)

    step_grad = urow[...] + exact(fade * qcol[...], eye, TN)
    gs_ref[...] = step_grad
    at_end = jnp.sum(exact(scale * qcol[...], eye, TN), axis=1, keepdims=True)
    at_end += jnp.exp(run_row[:, TOK - 1 : TOK]) * inner_hq
    gd_ref[...] = exact(exact(dcol[...], eye, TN) - dt_row * step_grad, lower, NN) + at_end

    finish(gcs, gc_ref, ac_s, ac_r)
    finish(gbs, gb_ref, ab_s, ab_r)

    for copy in sent:
        copy.wait_send()
    for i in range(2):
        q_part(i).wait_send()

    @pl.when(jnp.logical_not(stays))
    def _():
        inside.wait_send()

    for is_odd in range(2):

        @pl.when(odd == is_odd)
        def _():
            for stage in range(2):
                for way in range(2):
                    for group in range(2):
                        z_hop(way, stage, group, is_odd).wait_send()


def closing(h, lane, lane1, b_all, x_ref, gy, dxs, hbuf, qbuf, qcol, scale, skip_ref, gi_ref, inner_hq):
    ch = slice(h * WIDTH, (h + 1) * WIDTH)
    grad = qbuf[2 * h : 2 * h + 2].reshape(WIDTH, STATE)
    part, rest = split(grad)
    fed = mm(b_all, part, NT) + mm(b_all, rest, NT)
    met = jnp.sum(x_ref[:, ch].astype(F32) * fed, axis=1, keepdims=True)
    qcol[...] += jnp.where(lane == h, met, 0.0)
    gi_ref[:, ch] = (
        dxs[:, ch]
        + skip_ref[:, h : h + 1] * gy[:, ch].astype(F32)
        + scale[:, h : h + 1] * fed
    ).astype(BF16)
    state = hbuf[2 * h : 2 * h + 2].reshape(WIDTH, STATE)
    prod = state * grad
    total = jnp.sum(jnp.sum(prod, axis=0, keepdims=True), axis=1, keepdims=True)
    return inner_hq + jnp.where(lane1 == h, total, 0.0)


def hand_over(*refs):
    given, out, room, sems = refs[:5], refs[5:10], refs[10:15], refs[15]
    come = [pltpu.make_async_copy(given[i], room[i], sems.at[i]) for i in range(5)]
    leave = [pltpu.make_async_copy(room[i], out[i], sems.at[5 + i]) for i in range(5)]
    for copy in come:
        copy.start()
    for i in range(5):
        come[i].wait()
        leave[i].start()
    for copy in leave:
        copy.wait()


def local(grad_out, out_weight, ssm_input, step_size, log_decay, b_in, c_in, skip):
    vmem = pl.BlockSpec(memory_space=pltpu.VMEM)
    here = pl.BlockSpec(memory_space=pl.ANY)
    dma = pltpu.SemaphoreType.DMA
    slices = pltpu.VMEM((GROUP, SLICE, STATE), F32)
    halves = pltpu.VMEM((CHIPS, SLICE, STATE), F32)
    tagged = pltpu.VMEM((CHIPS, SLICE + 8, STATE), F32)
    short_parts = pltpu.VMEM((GROUP, PART, STATE), BF16)
    short_square = pltpu.VMEM((TOK, STATE), BF16)
    by_row = pltpu.VMEM((HEADS, TOK), F32)
    sums = pltpu.VMEM((CHUNKS, TOK, WIDE), F32)
    short = pltpu.VMEM((CHUNKS, TOK, WIDE), BF16)
    by_head = pltpu.VMEM((TOK, HEADS), F32)
    wide = pltpu.VMEM((TOK, ROWS), BF16)
    peers = dma((GROUP,))
    gi, gs, gd, gb, gc = pl.pallas_call(
        kernel,
        out_shape=(
            jax.ShapeDtypeStruct((TOK, ROWS), BF16),
            jax.ShapeDtypeStruct((HEADS, TOK), F32),
            jax.ShapeDtypeStruct((HEADS, TOK), F32),
            jax.ShapeDtypeStruct((TOK, STATE), F32),
            jax.ShapeDtypeStruct((TOK, STATE), F32),
        ),
        in_specs=[here] * 8,
        out_specs=[vmem] * 5,
        scratch_shapes=[
            wide,
            by_row, by_row,
            pltpu.VMEM((TOK, STATE), BF16), pltpu.VMEM((TOK, STATE), BF16),
            pltpu.VMEM((1, HEADS), F32),
            dma((7,)),
            pltpu.VMEM((4, ROWS, COLS), BF16),
            pltpu.VMEM((8, 2, TOK, COLS), BF16),
            pltpu.VMEM((CHUNKS, 2, TOK, WIDE), F32), pltpu.VMEM((CHUNKS, 2, TOK, WIDE), F32),
            sums, sums, short, short,
            wide,
            wide, wide,
            wide, wide,
            pltpu.VMEM((2, TOK, TOK), BF16),
            pltpu.VMEM((TOK, ROWS), F32),
            pltpu.VMEM((TOK, TOK), F32),
            pltpu.VMEM((TOK, TOK), F32),
            pltpu.VMEM((HEADS, TOK), F32),
            by_head,
            by_head,
            pltpu.VMEM((HEADS, 8, 128), F32),
            pltpu.VMEM((HEADS, 8, 128), F32),
            slices, halves, tagged, tagged, halves, halves, halves, slices,
            slices, halves, halves, halves, halves, halves, halves, slices,
            short_square, short_square,
            short_parts, short_parts,
            short_square, short_square,
            dma((len(HOPS),)), dma((len(HOPS),)),
            dma((3,)), dma((2, 2)),
            dma((2, 2, 2)), dma((2, 2, 2)),
            dma((CHUNKS,)), dma((CHUNKS,)),
            dma((CHUNKS,)), dma((CHUNKS,)),
            dma((CHUNKS,)), dma((CHUNKS,)),
        ] + [peers] * 18,
        compiler_params=pltpu.CompilerParams(
            collective_id=0, has_side_effects=True, vmem_limit_bytes=60 * 2**20
        ),
        name="layer_backward",
    )(
        grad_out, out_weight, ssm_input, step_size.T, log_decay.T, b_in, c_in, skip.reshape(1, HEADS)
    )
    gi, gs, gd, gb, gc = pl.pallas_call(
        hand_over,
        out_shape=tuple(jax.ShapeDtypeStruct(a.shape, a.dtype) for a in (gi, gs, gd, gb, gc)),
        in_specs=[here] * 5,
        out_specs=[here] * 5,
        scratch_shapes=[pltpu.VMEM(a.shape, a.dtype) for a in (gi, gs, gd, gb, gc)] + [dma((10,))],
        name="hand_over",
    )(gi, gs, gd, gb, gc)
    return gi, gs.T, gd.T, gb, gc


def solution(mesh):
    in_specs = (
        P("seq", "head"),
        P("head", "seq"),
        P("seq", "head"),
        P("seq", "head"),
        P("seq", "head"),
        P("seq", None),
        P("seq", None),
        P("head"),
    )
    out_specs = (
        P("seq", "head"),
        P("seq", "head"),
        P("seq", "head"),
        P("seq", None),
        P("seq", None),
    )
    return jax.shard_map(local, mesh=mesh, in_specs=in_specs, out_specs=out_specs, check_vma=False)
```
